1024 devices in a mesh: gx: 32 (over y, z_hi, core), gy: 4 (over z_lo), gz: 8 (over x).
Axes of the slice: x: 8, y: 8, z: 8 (z_hi: 2, z_lo: 4; z = z_hi * 4 + z_lo), core: 2. Of those that a mesh axis runs over, the one named last changes fastest.
Arguments:
- les_state: float32 [5, 256, 32, 1024], P(None, 'gx', 'gy', 'gz'), may hold values from -0.4 to 0.4
- acoustic_state: float32 [4, 256, 32, 1024], P(None, 'gx', 'gy', 'gz'), may hold values from -0.04 to 0.04
- mean_flow: float32 [3, 256, 32, 1024], P(None, 'gx', 'gy', 'gz'), may hold values from -0.5 to 0.5
- projection: float32 [8, 8], replicated, may hold values from -0.3 to 1.3, as said below
- target_owner: int32 [32, 4, 128], P('gx', 'gy', 'gz'), may hold values from 0 to 31, as said below
- target_slot: int32 [32, 4, 128], P('gx', 'gy', 'gz'), may hold values from 0 to 15
Outputs:
- les_next: float32 [5, 256, 32, 1024], P(None, 'gx', 'gy', 'gz')
- source_nodes: float32 [3, 256, 32, 1024], P(None, 'gx', 'gy', 'gz')
- acoustic_next: float32 [4, 256, 32, 1024], P(None, 'gx', 'gy', 'gz')
The draws below stay inside these ranges and needn't reach their ends.
Inputs may be any that keep to these rules, and one draw needn't show every extreme that they name: `target_owner`: the blocks of the device with index i along gx name as owners exactly the 4 consecutive indices from (i * (32 - 3)) // 32 on, each for exactly 4 blocks. `projection`: diagonal entries lie in 0.7 to 1.3, the others in -0.3 to 0.3.
All inputs are finite; a program needn't handle non-finite values.
Results may differ from the reference program's by a relative error of at most 0.00011.
Values sent between devices are 32-bit elements; how exact they have to be, the bound alone decides.
A program may use at most 32 MiB of HBM per device.

```python
import jax
import jax.numpy as jnp
import numpy as np
from jax import lax

CX = 8
CY = 8
CZ = 128
EX = 1
EY = 1
EZ = 16
NX = 256
NY = 32
NZ = 1024
NAX = 256
NAY = 32
NAZ = 1024
N_GX = 32
N_GY = 4
N_GZ = 8


def draw_projection(key, part):
    diagonal_key, spread_key = jax.random.split(key)
    diagonal = jax.random.uniform(diagonal_key, (8,), jnp.float32, 0.8, 1.2)
    spread = jax.random.uniform(spread_key, (8, 8), jnp.float32, -0.25, 0.25)
    identity = jnp.eye(8, dtype=jnp.float32)
    return spread * (1.0 - identity) + identity * diagonal[:, None]


def draw_target_owner(key, part):
    count_x = NX // CX
    count_y = NY // CY
    count_z = NZ // CZ
    blocks_x = CX // 8
    blocks_y = CY // 8
    blocks_z = CZ // 8
    block_total = blocks_x * blocks_y * blocks_z
    window = min(4, count_x)
    capacity = block_total // window
    device_keys = jax.random.split(jax.random.fold_in(key, 17), count_x * count_y * count_z)
    ranks = jax.vmap(lambda device_key: jax.random.permutation(device_key, block_total))(device_keys)
    ranks = ranks.reshape(count_x, count_y, count_z, block_total).astype(jnp.int32)
    device_x = jnp.arange(count_x, dtype=jnp.int32)[:, None, None, None]
    start_owner = device_x * (count_x - window + 1) // count_x
    owners = start_owner + ranks // capacity
    owners = owners.reshape(count_x, count_y, count_z, blocks_x, blocks_y, blocks_z).transpose(0, 3, 1, 4, 2, 5)
    return owners.reshape(count_x * blocks_x, count_y * blocks_y, count_z * blocks_z).astype(jnp.int32)


def set_ends(entries, own_key, least, top_value):
    shape = entries.shape
    place = [jax.random.randint(jax.random.fold_in(own_key, axis), (), 0, shape[axis]) for axis in range(len(shape))]
    entries = entries.at[tuple(place)].set(least)
    longest = shape.index(max(shape))
    place[longest] = (place[longest] + 1) % shape[longest]
    return entries.at[tuple(place)].set(top_value)


def level_of(own_key, shape, cuts, low, largest):
    def one(axis_at, parts):
        draws = jax.random.uniform(jax.random.fold_in(jax.random.fold_in(own_key, 6), axis_at), (parts,), jnp.float32, low / len(cuts), largest / len(cuts))
        return jnp.repeat(jnp.exp(draws), shape[axis_at] // parts).reshape((-1,) + (1,) * (len(shape) - axis_at - 1))

    factor_of = one(*cuts[0])
    for cut in cuts[1:]:
        factor_of = factor_of * one(*cut)
    return factor_of


def scatter_about(own_key, dims, deviation, bound, pieces=(), kind=jnp.bfloat16):
    drawn = deviation * jax.random.normal(own_key, dims, jnp.float32)
    if pieces:
        drawn = drawn * level_of(own_key, dims, pieces, -0.22, 0.18)
    return jnp.clip(drawn, -bound, bound).astype(kind)


def setup_inputs(seed: int = 0) -> dict:
    streams_of = jax.random.split(jax.random.key(seed), 7)
    les_state = jnp.clip(jax.random.uniform(streams_of[0], (5, NX, NY, NZ), jnp.float32, -0.4, 0.4) * level_of(streams_of[0], (5, NX, NY, NZ), ((1, 32), (2, 4), (3, 8)), -0.4, 0.0), -0.4, 0.4)
    acoustic_state = scatter_about(streams_of[1], (4, NAX, NAY, NAZ), 0.01, 0.04, ((1, 32), (2, 4), (3, 8)), jnp.float32)
    mean_flow = jnp.clip(jax.random.uniform(streams_of[2], (3, NAX, NAY, NAZ), jnp.float32, -0.5, 0.5) * level_of(streams_of[2], (3, NAX, NAY, NAZ), ((1, 32), (2, 4), (3, 8)), -0.4, 0.0), -0.5, 0.5)
    projection = draw_projection(jax.random.fold_in(streams_of[6], 71), 0)
    target_owner = draw_target_owner(jax.random.fold_in(streams_of[6], 71), 0)
    target_slot = set_ends(jax.random.randint(streams_of[5], (NX // 8, NY // 8, NZ // 8), 0, EX * EY * EZ), jax.random.fold_in(streams_of[5], 1), 0, (EX * EY * EZ) - 1).astype(jnp.int32)
    return dict(les_state=les_state, acoustic_state=acoustic_state, mean_flow=mean_flow, projection=projection, target_owner=target_owner, target_slot=target_slot)


lobatto_points = np.array([-1.0, -0.8717401485096066, -0.5917001814331423, -0.2092992179024789, 0.2092992179024789, 0.5917001814331423, 0.8717401485096066, 1.0])
flux_half = 0.08
viscous_ratio = 0.08
gamma_less = 0.4
acoustic_step = 0.01
upwind_speed = 1.5
face_lift = 28.0


def derivative_matrix():
    products = np.array([np.prod([lobatto_points[row_index] - lobatto_points[partner_index] for partner_index in range(8) if partner_index != row_index]) for row_index in range(8)])
    matrix = np.zeros((8, 8))
    for row_index in range(8):
        for col_index in range(8):
            if col_index != row_index:
                matrix[row_index, col_index] = products[row_index] / (products[col_index] * (lobatto_points[row_index] - lobatto_points[col_index]))
        matrix[row_index, row_index] = -np.sum(matrix[row_index])
    return matrix


def inner_slice(padded, axis_dim, offset):
    selector = [slice(None)]
    for dim_index in range(3):
        extent = padded.shape[dim_index + 1]
        if dim_index == axis_dim:
            selector.append(slice(1 + offset, extent - 1 + offset))
        else:
            selector.append(slice(1, extent - 1))
    return padded[tuple(selector)]


def full_state(padded):
    free_stream = jnp.array([1.0, 0.0, 0.0, 0.0, 2.5], jnp.float32)[:, None, None, None]
    return padded + free_stream


def les_rate(padded):
    state_full = full_state(padded)
    density = state_full[0]
    momentum = state_full[1:4]
    energy = state_full[4]
    velocity = momentum / density
    pressure = gamma_less * (energy - 0.5 * jnp.sum(momentum * velocity, axis=0))
    center = inner_slice(padded, 0, 0)
    change = jnp.zeros_like(center)
    for axis_dim in range(3):
        axis_speed = velocity[axis_dim]
        flux_rows = [momentum[axis_dim]]
        for component in range(3):
            term = momentum[component] * axis_speed
            if component == axis_dim:
                term = term + pressure
            flux_rows.append(term)
        flux_rows.append((energy + pressure) * axis_speed)
        fluxes = jnp.stack(flux_rows)
        change = change - flux_half * (inner_slice(fluxes, axis_dim, 1) - inner_slice(fluxes, axis_dim, -1))
        change = change + viscous_ratio * (inner_slice(padded, axis_dim, 1) + inner_slice(padded, axis_dim, -1) - 2.0 * center)
    return change


def lamb_vector(padded):
    state_full = full_state(padded)
    velocity = state_full[1:4] / state_full[0]

    def slope(component, axis_dim):
        return 0.5 * (inner_slice(velocity, axis_dim, 1)[component] - inner_slice(velocity, axis_dim, -1)[component])

    vort_x = slope(2, 1) - slope(1, 2)
    vort_y = slope(0, 2) - slope(2, 0)
    vort_z = slope(1, 0) - slope(0, 1)
    speed = inner_slice(velocity, 0, 0)
    return jnp.stack([vort_y * speed[2] - vort_z * speed[1], vort_z * speed[0] - vort_x * speed[2], vort_x * speed[1] - vort_y * speed[0]])


def project_blocks(lamb_field, projection):
    component_count, size_x, size_y, size_z = lamb_field.shape
    blocks = lamb_field.reshape(component_count, size_x // 8, 8, size_y // 8, 8, size_z // 8, 8).transpose(1, 3, 5, 0, 2, 4, 6)
    highest = lax.Precision.HIGHEST
    blocks = jnp.einsum('ia,xyzcabe->xyzcibe', projection, blocks, precision=highest)
    blocks = jnp.einsum('jb,xyzcibe->xyzcije', projection, blocks, precision=highest)
    blocks = jnp.einsum('ke,xyzcije->xyzcijk', projection, blocks, precision=highest)
    return blocks.reshape(size_x // 8, size_y // 8, size_z // 8, component_count * 512)


def flux_along(state_now, mean_speed, axis_dim):
    pressure = state_now[0]
    axis_speed = mean_speed[axis_dim]
    flux_rows = [axis_speed * pressure + state_now[1 + axis_dim]]
    for component in range(3):
        term = axis_speed * state_now[1 + component]
        if component == axis_dim:
            term = term + pressure
        flux_rows.append(term)
    return jnp.stack(flux_rows)


def element_derivative(field_data, axis_dim):
    deriv_table = jnp.asarray(derivative_matrix(), jnp.float32)
    moved_field = jnp.moveaxis(field_data, axis_dim + 1, -1)
    lead_shape = moved_field.shape[:-1]
    extent = moved_field.shape[-1]
    grouped = moved_field.reshape(lead_shape + (extent // 8, 8))
    result_data = jnp.einsum('...k,jk->...j', grouped, deriv_table, precision=lax.Precision.HIGHEST)
    return jnp.moveaxis(result_data.reshape(lead_shape + (extent,)), -1, axis_dim + 1)


def acoustic_rate(padded, mean_speed, source):
    center = inner_slice(padded, 0, 0)
    total_rate = jnp.zeros_like(center)
    for axis_dim in range(3):
        extent = center.shape[axis_dim + 1]
        position = jnp.arange(extent) % 8
        shape_list = [1, 1, 1, 1]
        shape_list[axis_dim + 1] = extent
        right_face = (position == 7).astype(jnp.float32).reshape(shape_list)
        left_face = (position == 0).astype(jnp.float32).reshape(shape_list)
        upper_jump = inner_slice(padded, axis_dim, 1) - center
        lower_jump = inner_slice(padded, axis_dim, -1) - center
        total_rate = total_rate - element_derivative(flux_along(center, mean_speed, axis_dim), axis_dim)
        total_rate = total_rate - right_face * face_lift * (0.5 * flux_along(upper_jump, mean_speed, axis_dim) - 0.5 * upwind_speed * upper_jump)
        total_rate = total_rate + left_face * face_lift * (0.5 * flux_along(lower_jump, mean_speed, axis_dim) + 0.5 * upwind_speed * lower_jump)
    return total_rate + jnp.concatenate([jnp.zeros_like(source[:1]), source], axis=0)


def reference(les_state, acoustic_state, mean_flow, projection, target_owner, target_slot):
    pad_width = ((0, 0), (1, 1), (1, 1), (1, 1))
    first_padded = jnp.pad(les_state, pad_width)
    first_rate = les_rate(first_padded)
    lamb_field = lamb_vector(first_padded)
    section_state = les_state + first_rate
    second_rate = les_rate(jnp.pad(section_state, pad_width))
    les_next = les_state + 0.5 * (first_rate + second_rate)
    coeffs = project_blocks(lamb_field, projection)
    grid_y = (jnp.arange(target_owner.shape[1]) // (CY // 8)).astype(jnp.int32)[None, :, None]
    grid_z = (jnp.arange(target_owner.shape[2]) // (CZ // 8)).astype(jnp.int32)[None, None, :]
    count_x = EX * N_GX
    count_y = EY * N_GY
    count_z = EZ * N_GZ
    element_x = target_owner * EX + target_slot // (EY * EZ)
    element_y = grid_y * EY + (target_slot // EZ) % EY
    element_z = grid_z * EZ + target_slot % EZ
    element_ids = ((element_x * count_y + element_y) * count_z + element_z).reshape(-1).astype(jnp.int32)
    element_sums = jax.ops.segment_sum(coeffs.reshape(-1, 1536), element_ids, num_segments=count_x * count_y * count_z)
    source_nodes = element_sums.reshape(count_x, count_y, count_z, 3, 8, 8, 8).transpose(3, 0, 4, 1, 5, 2, 6).reshape(3, count_x * 8, count_y * 8, count_z * 8)
    first_acoustic = acoustic_rate(jnp.pad(acoustic_state, pad_width), mean_flow, source_nodes)
    middle_state = acoustic_state + acoustic_step * first_acoustic
    second_acoustic = acoustic_rate(jnp.pad(middle_state, pad_width), mean_flow, source_nodes)
    acoustic_next = acoustic_state + 0.5 * acoustic_step * (first_acoustic + second_acoustic)
    return les_next, source_nodes, acoustic_next
```

```python
import functools

import jax
import jax.numpy as jnp
import numpy as np
from jax import lax
from jax.experimental import pallas as pl
from jax.experimental.pallas import tpu as pltpu
from jax.sharding import PartitionSpec as P

MESH = pl.DeviceIdType.MESH
F32 = jnp.float32
BF16 = jnp.bfloat16

lobatto_points = np.array(
    [
        -1.0,
        -0.8717401485096066,
        -0.5917001814331423,
        -0.2092992179024789,
        0.2092992179024789,
        0.5917001814331423,
        0.8717401485096066,
        1.0,
    ]
)
flux_half = 0.08
gamma_less = 0.4
acoustic_step = 0.01
upwind_speed = 1.5
face_lift = 28.0
REACH = 3
WINDOW = 4


def derivative_matrix():
    points = lobatto_points
    gaps = points[:, None] - points[None, :] + np.eye(8)
    products = np.prod(gaps, axis=1)
    matrix = products[:, None] / (products[None, :] * gaps)
    np.fill_diagonal(matrix, 0.0)
    np.fill_diagonal(matrix, -matrix.sum(axis=1))
    return matrix


def derivative_operands():
    deriv = derivative_matrix()
    eye = np.eye(8)
    along_xy = np.concatenate([np.kron(deriv, eye), np.kron(eye, deriv)], axis=1)
    along_z = np.kron(np.eye(16), deriv.T)
    whole = np.concatenate([along_xy, along_z], axis=0).astype(np.float32)
    high = whole.astype(jnp.bfloat16)
    low = (whole - high.astype(np.float32)).astype(jnp.bfloat16)
    return np.stack([high, low])


def split(value):
    high = value.astype(BF16)
    return high, (value - high.astype(F32)).astype(BF16)


def dot_nn(left, right):
    return lax.dot_general(left, right, (((1,), (0,)), ((), ())), preferred_element_type=F32)


def dot_nt(left, right):
    return lax.dot_general(left, right, (((1,), (1,)), ((), ())), preferred_element_type=F32)


def lanes(shape):
    return lax.broadcasted_iota(jnp.int32, shape, len(shape) - 1)


def rows(shape):
    return lax.broadcasted_iota(jnp.int32, shape, len(shape) - 2)


class Halo:
    def __init__(self, x_ref, y_ref, z_ref, first):
        self.x_ref, self.y_ref, self.z_ref, self.first = x_ref, y_ref, z_ref, first

    def face(self, component, axis, side):
        at = self.first + component
        if axis == 0:
            return self.x_ref[side, at]
        if axis == 1:
            return self.y_ref[side, at]
        face = self.z_ref[side]
        return [jnp.broadcast_to(face[:, 8 * at + x : 8 * at + x + 1], (8, 128)) for x in range(8)]

    def shifted(self, field, component, axis, side):
        return shift(field, self.face(component, axis, side), axis, side)


def shift(field, face, axis, side):
    if axis == 0:
        if side == 0:
            return jnp.concatenate([face[None], field[:-1]], axis=0)
        return jnp.concatenate([field[1:], face[None]], axis=0)
    if axis == 1:
        rolled = pltpu.roll(field, 1 if side == 0 else 7, 1)
        edge = rows((8, 8, 128)) == (0 if side == 0 else 7)
        return jnp.where(edge, jnp.broadcast_to(face[:, None, :], (8, 8, 128)), rolled)
    rolled = pltpu.roll(field, 1 if side == 0 else 127, 2)
    edge = lanes((8, 8, 128)) == (0 if side == 0 else 127)
    return jnp.where(edge, jnp.stack(face), rolled)


def les_rate(state, halo):
    total = [-6.0 * part for part in state]
    for axis in range(3):
        for side in range(2):
            near = [halo.shifted(state[c], c, axis, side) for c in range(5)]
            momentum = near[1:4]
            energy = near[4] + 2.5
            inverse = 1.0 / (near[0] + 1.0)
            square = (
                momentum[0] * momentum[0] + momentum[1] * momentum[1] + momentum[2] * momentum[2]
            )
            pressure = gamma_less * (energy - 0.5 * (square * inverse))
            speed = momentum[axis] * inverse
            flux = [momentum[axis]]
            for component in range(3):
                term = momentum[component] * speed
                flux.append(term + pressure if component == axis else term)
            flux.append((energy + pressure) * speed)
            for c in range(5):
                total[c] = total[c] + (near[c] + flux[c] if side == 0 else near[c] - flux[c])
    return [flux_half * part for part in total]


def lamb_vector(state, halo):
    inverse = 1.0 / (state[0] + 1.0)
    velocity = [state[1 + c] * inverse for c in range(3)]
    packed = []
    for side in range(2):
        face = halo.z_ref[side]
        inverse_face = 1.0 / (face + 1.0)
        packed.append([face * pltpu.roll(inverse_face, 8 * (1 + c), 1) for c in range(3)])

    def near(component, axis, side):
        if axis == 2:
            face = packed[side][component]
            start = 8 * (1 + component)
            face = [jnp.broadcast_to(face[:, start + x : start + x + 1], (8, 128)) for x in range(8)]
        else:
            face = halo.face(1 + component, axis, side) / (halo.face(0, axis, side) + 1.0)
        return shift(velocity[component], face, axis, side)

    def slope(component, axis):
        return 0.5 * (near(component, axis, 1) - near(component, axis, 0))

    vort_x = slope(2, 1) - slope(1, 2)
    vort_y = slope(0, 2) - slope(2, 0)
    vort_z = slope(1, 0) - slope(0, 1)
    return [
        vort_y * velocity[2] - vort_z * velocity[1],
        vort_z * velocity[0] - vort_x * velocity[2],
        vort_x * velocity[1] - vort_y * velocity[0],
    ]


def flux_along(state, mean_speed, axis):
    flux = [mean_speed[axis] * state[0] + state[1 + axis]]
    for component in range(3):
        term = mean_speed[axis] * state[1 + component]
        flux.append(term + state[0] if component == axis else term)
    return flux


def acoustic_rate(state, mean_speed, halo, deriv_ref):
    flux_x = flux_along(state, mean_speed, 0)
    flux_y = flux_along(state, mean_speed, 1)
    flux_z = flux_along(state, mean_speed, 2)
    high = deriv_ref[0]
    low = deriv_ref[1]
    columns = jnp.concatenate(
        [
            jnp.concatenate([flux_x[c].reshape(64, 128), flux_y[c].reshape(64, 128)], axis=0)
            for c in range(4)
        ],
        axis=1,
    )
    column_high, column_low = split(columns)
    slopes_xy = (
        dot_nn(high[:64], column_high) + dot_nn(high[:64], column_low) + dot_nn(low[:64], column_high)
    )
    lines = jnp.concatenate([flux_z[c].reshape(64, 128) for c in range(4)], axis=0)
    line_high, line_low = split(lines)
    slopes_z = (
        dot_nn(line_high, high[64:]) + dot_nn(line_low, high[64:]) + dot_nn(line_high, low[64:])
    )
    total = [
        -(slopes_xy[:, 128 * c : 128 * c + 128] + slopes_z[64 * c : 64 * c + 64]).reshape(8, 8, 128)
        for c in range(4)
    ]
    half_lift = 0.5 * face_lift
    upwind_lift = half_lift * upwind_speed
    for side in range(2):
        plane = 0 if side == 0 else 7
        jump = [halo.face(c, 0, side) - state[c][plane] for c in range(4)]
        flux = flux_along(jump, [mean_speed[0][plane], None, None], 0)
        sign = half_lift if side == 0 else -half_lift
        for c in range(4):
            lifted = (sign * flux[c] + upwind_lift * jump[c])[None]
            zeros = jnp.zeros((7, 8, 128), F32)
            parts = [lifted, zeros] if side == 0 else [zeros, lifted]
            total[c] = total[c] + jnp.concatenate(parts, axis=0)
    for axis in (1, 2):
        position = rows((8, 8, 128)) if axis == 1 else lanes((8, 8, 128)) % 8
        is_left, is_right = position == 0, position == 7
        jump = []
        for c in range(4):
            if axis == 1:
                lower = jnp.broadcast_to(halo.face(c, 1, 0)[:, None, :], (8, 8, 128))
                upper = jnp.broadcast_to(halo.face(c, 1, 1)[:, None, :], (8, 8, 128))
            else:
                lower = halo.shifted(state[c], c, 2, 0)
                upper = halo.shifted(state[c], c, 2, 1)
            other = jnp.where(is_left, lower, jnp.where(is_right, upper, state[c]))
            jump.append(other - state[c])
        flux = flux_along(jump, mean_speed, axis)
        sign = jnp.where(is_left, half_lift, -half_lift)
        for c in range(4):
            total[c] = total[c] + (sign * flux[c] + upwind_lift * jump[c])
    return total


def pack_faces_z(planes, side):
    face = jnp.zeros((8, 128), F32)
    lane = lanes((8, 128))
    at = 0 if side == 0 else 127
    for n, plane in enumerate(planes):
        face = jnp.where(lane == n, jnp.broadcast_to(plane[:, at : at + 1], (8, 128)), face)
    return face


def quarter_transpose(groups, target):
    lane = lanes(groups[0].shape) // 32
    result = None
    for g, group in enumerate(groups):
        moved = group if g == target else pltpu.roll(group, (32 * (g - target)) % 128, 1)
        result = moved if result is None else jnp.where(lane == g, moved, result)
    return result


def projection_operands(proj_ref):
    lane = lanes((8, 128))
    row = rows((8, 128))
    tile = jnp.zeros((8, 128), F32)
    for k in range(8):
        for e in range(8):
            tile = jnp.where((row == k) & (lane % 8 == e), proj_ref[k, e], tile)
    pieces = []
    for i in range(8):
        weight = jnp.zeros((8, 128), F32)
        for a in range(8):
            weight = jnp.where(lane % 64 // 8 == a, proj_ref[i, a], weight)
        pieces.append(weight * tile)
    return tile, jnp.concatenate(pieces, axis=0)


def place_operands(tile, own_ref, slot_ref, start):
    lane = lanes((8, 128))
    row = rows((8, 128))
    block = lane // 8
    owner = jnp.zeros((8, 128), jnp.int32)
    slot = jnp.zeros((8, 128), jnp.int32)
    for b in range(16):
        owner = jnp.where(block == b, own_ref[0, 0, b], owner)
        slot = jnp.where(block == b, slot_ref[0, 0, b], slot)
    rank = jnp.zeros((8, 128), jnp.int32)
    for b in range(16):
        rank = rank + jnp.where((owner == own_ref[0, 0, b]) & (block > b), 1, 0)
    place = (owner - start) * WINDOW + rank
    columns = jnp.concatenate([jnp.where(place == n, tile, 0.0) for n in range(16)], axis=0)
    same = (lane % 8) == row
    picks = jnp.concatenate(
        [jnp.where((place == n) & same, 1.0, 0.0) for n in range(16)], axis=0
    )
    labels = dot_nt(slot.astype(F32).astype(BF16), picks.astype(BF16))
    return columns, labels


def kernel(
    sizes,
    les,
    ac,
    mf,
    proj,
    own,
    slot,
    deriv,
    les_out,
    src_out,
    ac_out,
    les_v,
    ac_v,
    mf_v,
    deriv_v,
    send_y,
    send_z,
    halo_x,
    halo_y,
    halo_z,
    pieces,
    arrived,
    sec_v,
    sec_send_y,
    sec_send_z,
    sec_halo_x,
    sec_halo_y,
    sec_halo_z,
    mid_v,
    mid_send_y,
    mid_send_z,
    mid_halo_x,
    mid_halo_y,
    mid_halo_z,
    rate_v,
    slope_v,
    les_next,
    src_v,
    ac_next,
    load_sem,
    out_sem,
    send_sem,
    recv_sem,
    piece_send,
    piece_recv,
):
    names = ("gx", "gy", "gz")
    at = [lax.axis_index(name) for name in names]
    me = at[0]
    count_x = sizes[0]

    def exists(axis, distance):
        other = at[axis] + distance
        return (other >= 0) & (other < sizes[axis])

    barrier = pltpu.get_barrier_semaphore()
    expected = jnp.int32(0)
    for axis, reach in ((0, REACH), (1, 1), (2, 1)):
        for distance in range(-reach, reach + 1):
            if distance == 0:
                continue
            near = exists(axis, distance)

            @pl.when(near)
            def _():
                pl.semaphore_signal(
                    barrier,
                    inc=1,
                    device_id={names[axis]: at[axis] + distance},
                    device_id_type=MESH,
                )

            expected = expected + jnp.where(near, 1, 0)

    loads = [
        pltpu.make_async_copy(source, target, load_sem.at[n])
        for n, (source, target) in enumerate(
            ((les, les_v), (ac, ac_v), (mf, mf_v), (deriv, deriv_v))
        )
    ]
    for load in loads:
        load.start()

    def start_of(index):
        return (index * (count_x - (WINDOW - 1))) // count_x

    start = start_of(me)

    def comes(distance):
        other = me + distance
        begin = start_of(other)
        return exists(0, distance) & (begin <= me) & (me < begin + WINDOW)

    for side, distance in ((0, -1), (1, 1)):
        for axis, refs in (
            (0, (halo_x, sec_halo_x, mid_halo_x)),
            (1, (halo_y, sec_halo_y, mid_halo_y)),
            (2, (halo_z, sec_halo_z, mid_halo_z)),
        ):

            @pl.when(jnp.logical_not(exists(axis, distance)))
            def _():
                for ref in refs:
                    ref[side] = jnp.zeros(ref.shape[1:], F32)

    for distance in range(-REACH, REACH + 1):
        if distance != 0:

            @pl.when(jnp.logical_not(comes(distance)))
            def _():
                arrived[distance + REACH] = jnp.zeros((56, 128), F32)

    def message(source, target, axis, side, slot_index):
        distance = -1 if side == 0 else 1
        return pltpu.make_async_remote_copy(
            src_ref=source,
            dst_ref=target,
            send_sem=send_sem.at[slot_index],
            recv_sem=recv_sem.at[slot_index],
            device_id={names[axis]: at[axis] + distance},
            device_id_type=MESH,
        )

    def begin(entries):
        for source, target, axis, side, slot_index in entries:

            @pl.when(exists(axis, -1 if side == 0 else 1))
            def _():
                message(source, target, axis, side, slot_index).start()

    def arrive(entries):
        for source, target, axis, side, slot_index in entries:
            @pl.when(exists(axis, 1 if side == 0 else -1))
            def _():
                message(source, target, axis, side, slot_index).wait_recv()

    def drain(entries):
        for source, target, axis, side, slot_index in entries:

            @pl.when(exists(axis, -1 if side == 0 else 1))
            def _():
                message(source, target, axis, side, slot_index).wait_send()

    flow_x = [
        (les.at[:, 0 if side == 0 else 7], halo_x.at[1 - side, 0:5], 0, side, side)
        for side in range(2)
    ]
    sound_x = [
        (ac.at[:, 0 if side == 0 else 7], halo_x.at[1 - side, 5:9], 0, side, 2 + side)
        for side in range(2)
    ]
    near_yz = [
        (send_y.at[side], halo_y.at[1 - side], 1, side, 4 + side) for side in range(2)
    ] + [(send_z.at[side], halo_z.at[1 - side], 2, side, 6 + side) for side in range(2)]
    section = (
        [
            (sec_v.at[:, 0 if side == 0 else 7], sec_halo_x.at[1 - side], 0, side, 8 + side)
            for side in range(2)
        ]
        + [
            (sec_send_y.at[side], sec_halo_y.at[1 - side], 1, side, 10 + side)
            for side in range(2)
        ]
        + [
            (sec_send_z.at[side], sec_halo_z.at[1 - side], 2, side, 12 + side)
            for side in range(2)
        ]
    )
    middle = (
        [
            (mid_v.at[:, 0 if side == 0 else 7], mid_halo_x.at[1 - side], 0, side, 14 + side)
            for side in range(2)
        ]
        + [
            (mid_send_y.at[side], mid_halo_y.at[1 - side], 1, side, 16 + side)
            for side in range(2)
        ]
        + [
            (mid_send_z.at[side], mid_halo_z.at[1 - side], 2, side, 18 + side)
            for side in range(2)
        ]
    )

    for load in loads[:2]:
        load.wait()
    for side in range(2):
        row = 0 if side == 0 else 7
        send_y[side, 0:5] = les_v[:, :, row, :]
        send_y[side, 5:9] = ac_v[:, :, row, :]
        send_z[side] = pack_faces_z(
            [les_v[c, x] for c in range(5) for x in range(8)]
            + [ac_v[c, x] for c in range(4) for x in range(8)],
            side,
        )

    pl.semaphore_wait(barrier, expected)
    begin(flow_x)
    begin(near_yz)
    begin(sound_x)

    tile, plane_weights = projection_operands(proj)
    weight_high, weight_low = split(plane_weights)
    plane_operand = jnp.concatenate([weight_high, weight_low], axis=1)
    columns, labels = place_operands(tile, own, slot, start)
    column_high, column_low = split(columns)
    column_operand = jnp.concatenate(
        [
            jnp.concatenate([column_high, column_high], axis=1),
            jnp.concatenate([column_low, column_low], axis=1),
        ],
        axis=0,
    )
    for w in range(WINDOW):
        pieces[w, 48:56] = quarter_transpose([labels] * 4, w)
    for load in loads[2:]:
        load.wait()

    state = [les_v[c] for c in range(5)]
    halo = Halo(halo_x, halo_y, halo_z, 0)
    arrive(near_yz)
    arrive(flow_x)
    lamb = lamb_vector(state, halo)
    cells = jnp.concatenate([part.reshape(64, 128) for part in lamb], axis=1)
    cell_high, cell_low = split(cells)
    stacked = jnp.concatenate([cell_high, cell_low, cell_high, cell_low], axis=0)
    planes = dot_nn(plane_operand, stacked)
    planes = jnp.concatenate([planes[:, 128 * c : 128 * c + 128] for c in range(3)], axis=0)
    plane_high, plane_low = split(planes)
    both = dot_nt(jnp.concatenate([plane_high, plane_low], axis=1), column_operand)
    placed = both[:, :128] + both[:, 128:]
    groups = [placed[48 * g : 48 * g + 48] for g in range(4)]
    for w in range(WINDOW):
        pieces[w, 0:48] = quarter_transpose(groups, w)

    def piece_copy(w):
        target = start + w
        slot_index = me - target + REACH
        return pltpu.make_async_remote_copy(
            src_ref=pieces.at[w],
            dst_ref=arrived.at[slot_index],
            send_sem=piece_send.at[w],
            recv_sem=piece_recv.at[slot_index],
            device_id={"gx": target},
            device_id_type=MESH,
        )

    for w in range(WINDOW):

        @pl.when(start + w != me)
        def _():
            piece_copy(w).start()

    arrived[REACH] = pieces[me - start]

    rate = les_rate(state, halo)
    for c in range(5):
        rate_v[c] = rate[c]
        sec_v[c] = state[c] + rate[c]
    for side in range(2):
        sec_send_y[side] = sec_v[:, :, 0 if side == 0 else 7, :]
        sec_send_z[side] = pack_faces_z(
            [sec_v[c, x] for c in range(5) for x in range(8)], side
        )
    begin(section)

    mean_speed = [mf_v[c] for c in range(3)]
    arrive(sound_x)
    sound = [ac_v[c] for c in range(4)]
    slopes = acoustic_rate(sound, mean_speed, Halo(halo_x, halo_y, halo_z, 5), deriv_v)
    for c in range(4):
        slope_v[c] = slopes[c]

    for distance in range(-REACH, REACH + 1):
        if distance != 0:

            @pl.when(comes(distance))
            def _():
                pltpu.make_async_remote_copy(
                    src_ref=pieces.at[0],
                    dst_ref=arrived.at[distance + REACH],
                    send_sem=piece_send.at[0],
                    recv_sem=piece_recv.at[distance + REACH],
                    device_id={"gx": me + distance},
                    device_id_type=MESH,
                ).wait_recv()

    halves = []
    tags = []
    zero = jnp.zeros((48, 128), F32)
    for half in range(2):
        members = [4 * half + n for n in range(4)]
        parts = [arrived[n, 0:48] if n < 7 else zero for n in members]
        quarter = [quarter_transpose(parts, g) for g in range(4)]
        halves.append(jnp.concatenate(quarter, axis=0))
        tag = jnp.zeros((8, 128), F32)
        for n in members:
            if n < 7:
                tag = jnp.where(lanes((8, 128)) // 32 == n % 4, arrived[n, 48:56], tag)
        tags.append(tag)
    same = (lanes((8, 128)) % 8) == rows((8, 128))
    picks = jnp.concatenate(
        [
            jnp.concatenate(
                [jnp.where((tag == float(s)) & same, 1.0, 0.0) for s in range(16)], axis=0
            )
            for tag in tags
        ],
        axis=1,
    ).astype(BF16)
    gathered = jnp.concatenate(halves, axis=1)
    gathered_high, gathered_low = split(gathered)
    source = dot_nt(gathered_high, picks) + dot_nt(gathered_low, picks)
    source = source.reshape(3, 8, 8, 128)
    src_v[...] = source
    for c in range(4):
        if c > 0:
            slope_v[c] = slope_v[c] + src_v[c - 1]
        mid_v[c] = ac_v[c] + acoustic_step * slope_v[c]
    for side in range(2):
        mid_send_y[side] = mid_v[:, :, 0 if side == 0 else 7, :]
        mid_send_z[side] = pack_faces_z(
            [mid_v[c, x] for c in range(4) for x in range(8)], side
        )
    begin(middle)
    src_copy = pltpu.make_async_copy(src_v, src_out, out_sem.at[1])
    src_copy.start()

    arrive(section)
    rate = les_rate([sec_v[c] for c in range(5)], Halo(sec_halo_x, sec_halo_y, sec_halo_z, 0))
    for c in range(5):
        les_next[c] = les_v[c] + 0.5 * (rate_v[c] + rate[c])
    les_copy = pltpu.make_async_copy(les_next, les_out, out_sem.at[0])
    les_copy.start()

    arrive(middle)
    slopes = acoustic_rate(
        [mid_v[c] for c in range(4)],
        [mf_v[c] for c in range(3)],
        Halo(mid_halo_x, mid_halo_y, mid_halo_z, 0),
        deriv_v,
    )
    for c in range(4):
        total = slope_v[c] + slopes[c]
        if c > 0:
            total = total + src_v[c - 1]
        ac_next[c] = ac_v[c] + 0.5 * acoustic_step * total
    ac_copy = pltpu.make_async_copy(ac_next, ac_out, out_sem.at[2])
    ac_copy.start()

    drain(flow_x)
    drain(sound_x)
    drain(near_yz)
    drain(section)
    drain(middle)
    for w in range(WINDOW):

        @pl.when(start + w != me)
        def _():
            piece_copy(w).wait_send()

    src_copy.wait()
    les_copy.wait()
    ac_copy.wait()


def local(les_state, acoustic_state, mean_flow, projection, target_owner, target_slot):
    sizes = tuple(lax.axis_size(name) for name in ("gx", "gy", "gz"))
    deriv = jnp.asarray(derivative_operands())
    anywhere = pl.BlockSpec(memory_space=pl.ANY)
    scalars = pl.BlockSpec(memory_space=pltpu.SMEM)

    def vmem(*shape):
        return pltpu.VMEM(shape, F32)

    def halos(n):
        return [vmem(2, n, 8, 128), vmem(2, n, 8, 128), vmem(2, 8, 128)]

    field = (8, 8, 128)
    return pl.pallas_call(
        functools.partial(kernel, sizes),
        name="coupled_step",
        out_shape=(
            jax.ShapeDtypeStruct((5,) + field, F32),
            jax.ShapeDtypeStruct((3,) + field, F32),
            jax.ShapeDtypeStruct((4,) + field, F32),
        ),
        in_specs=[anywhere, anywhere, anywhere, scalars, scalars, scalars, anywhere],
        out_specs=(anywhere, anywhere, anywhere),
        scratch_shapes=[
            vmem(5, *field),
            vmem(4, *field),
            vmem(3, *field),
            pltpu.VMEM((2, 192, 128), BF16),
            vmem(2, 9, 8, 128),
            vmem(2, 8, 128),
            *halos(9),
            vmem(4, 56, 128),
            vmem(7, 56, 128),
            vmem(5, *field),
            vmem(2, 5, 8, 128),
            vmem(2, 8, 128),
            *halos(5),
            vmem(4, *field),
            vmem(2, 4, 8, 128),
            vmem(2, 8, 128),
            *halos(4),
            vmem(5, *field),
            vmem(4, *field),
            vmem(5, *field),
            vmem(3, *field),
            vmem(4, *field),
            pltpu.SemaphoreType.DMA((4,)),
            pltpu.SemaphoreType.DMA((3,)),
            pltpu.SemaphoreType.DMA((20,)),
            pltpu.SemaphoreType.DMA((20,)),
            pltpu.SemaphoreType.DMA((4,)),
            pltpu.SemaphoreType.DMA((7,)),
        ],
        compiler_params=pltpu.CompilerParams(collective_id=0, has_side_effects=True),
    )(les_state, acoustic_state, mean_flow, projection, target_owner, target_slot, deriv)


def solution(mesh):
    fields = P(None, "gx", "gy", "gz")
    blocks = P("gx", "gy", "gz")
    return jax.shard_map(
        local,
        mesh=mesh,
        in_specs=(fields, fields, fields, P(), blocks, blocks),
        out_specs=(fields, fields, fields),
        check_vma=False,
    )
```

```python
import functools

import jax
import jax.numpy as jnp
import numpy as np
from jax import lax
from jax.experimental import pallas as pl
from jax.experimental.pallas import tpu as pltpu
from jax.sharding import PartitionSpec as P

MESH = pl.DeviceIdType.MESH
F32 = jnp.float32
BF16 = jnp.bfloat16

lobatto_points = np.array(
    [
        -1.0,
        -0.8717401485096066,
        -0.5917001814331423,
        -0.2092992179024789,
        0.2092992179024789,
        0.5917001814331423,
        0.8717401485096066,
        1.0,
    ]
)
flux_half = 0.08
gamma_less = 0.4
acoustic_step = 0.01
upwind_speed = 1.5
face_lift = 28.0
REACH = 3
WINDOW = 4


def derivative_matrix():
    points = lobatto_points
    gaps = points[:, None] - points[None, :] + np.eye(8)
    products = np.prod(gaps, axis=1)
    matrix = products[:, None] / (products[None, :] * gaps)
    np.fill_diagonal(matrix, 0.0)
    np.fill_diagonal(matrix, -matrix.sum(axis=1))
    return matrix


def derivative_operands():
    deriv = derivative_matrix()
    eye = np.eye(8)
    along_xy = np.concatenate([np.kron(deriv, eye), np.kron(eye, deriv)], axis=1)
    along_z = np.kron(np.eye(16), deriv.T)
    whole = np.concatenate([along_xy, along_z], axis=0).astype(np.float32)
    high = whole.astype(jnp.bfloat16)
    low = (whole - high.astype(np.float32)).astype(jnp.bfloat16)
    return np.stack([high, low])


def split(value):
    high = value.astype(BF16)
    return high, (value - high.astype(F32)).astype(BF16)


def dot_nn(left, right):
    return lax.dot_general(left, right, (((1,), (0,)), ((), ())), preferred_element_type=F32)


def dot_nt(left, right):
    return lax.dot_general(left, right, (((1,), (1,)), ((), ())), preferred_element_type=F32)


def lanes(shape):
    return lax.broadcasted_iota(jnp.int32, shape, len(shape) - 1)


def rows(shape):
    return lax.broadcasted_iota(jnp.int32, shape, len(shape) - 2)


class Halo:
    def __init__(self, x_ref, y_ref, z_ref, first):
        self.x_ref, self.y_ref, self.z_ref, self.first = x_ref, y_ref, z_ref, first

    def face(self, component, axis, side):
        at = self.first + component
        if axis == 0:
            return self.x_ref[side, at]
        if axis == 1:
            return self.y_ref[side, at]
        face = self.z_ref[side]
        return [jnp.broadcast_to(face[:, 8 * at + x : 8 * at + x + 1], (8, 128)) for x in range(8)]

    def shifted(self, field, component, axis, side):
        return shift(field, self.face(component, axis, side), axis, side)


def shift(field, face, axis, side):
    if axis == 0:
        if side == 0:
            return jnp.concatenate([face[None], field[:-1]], axis=0)
        return jnp.concatenate([field[1:], face[None]], axis=0)
    if axis == 1:
        rolled = pltpu.roll(field, 1 if side == 0 else 7, 1)
        edge = rows((8, 8, 128)) == (0 if side == 0 else 7)
        return jnp.where(edge, jnp.broadcast_to(face[:, None, :], (8, 8, 128)), rolled)
    rolled = pltpu.roll(field, 1 if side == 0 else 127, 2)
    edge = lanes((8, 8, 128)) == (0 if side == 0 else 127)
    return jnp.where(edge, jnp.stack(face), rolled)


def les_rate(state, halo):
    total = [-6.0 * part for part in state]
    for axis in range(3):
        for side in range(2):
            near = [halo.shifted(state[c], c, axis, side) for c in range(5)]
            momentum = near[1:4]
            energy = near[4] + 2.5
            inverse = 1.0 / (near[0] + 1.0)
            square = (
                momentum[0] * momentum[0] + momentum[1] * momentum[1] + momentum[2] * momentum[2]
            )
            pressure = gamma_less * (energy - 0.5 * (square * inverse))
            speed = momentum[axis] * inverse
            flux = [momentum[axis]]
            for component in range(3):
                term = momentum[component] * speed
                flux.append(term + pressure if component == axis else term)
            flux.append((energy + pressure) * speed)
            for c in range(5):
                total[c] = total[c] + (near[c] + flux[c] if side == 0 else near[c] - flux[c])
    return [flux_half * part for part in total]


def lamb_vector(state, halo):
    inverse = 1.0 / (state[0] + 1.0)
    velocity = [state[1 + c] * inverse for c in range(3)]
    packed = []
    for side in range(2):
        face = halo.z_ref[side]
        inverse_face = 1.0 / (face + 1.0)
        packed.append([face * pltpu.roll(inverse_face, 8 * (1 + c), 1) for c in range(3)])

    def near(component, axis, side):
        if axis == 2:
            face = packed[side][component]
            start = 8 * (1 + component)
            face = [jnp.broadcast_to(face[:, start + x : start + x + 1], (8, 128)) for x in range(8)]
        else:
            face = halo.face(1 + component, axis, side) / (halo.face(0, axis, side) + 1.0)
        return shift(velocity[component], face, axis, side)

    def slope(component, axis):
        return 0.5 * (near(component, axis, 1) - near(component, axis, 0))

    vort_x = slope(2, 1) - slope(1, 2)
    vort_y = slope(0, 2) - slope(2, 0)
    vort_z = slope(1, 0) - slope(0, 1)
    return [
        vort_y * velocity[2] - vort_z * velocity[1],
        vort_z * velocity[0] - vort_x * velocity[2],
        vort_x * velocity[1] - vort_y * velocity[0],
    ]


def flux_along(state, mean_speed, axis):
    flux = [mean_speed[axis] * state[0] + state[1 + axis]]
    for component in range(3):
        term = mean_speed[axis] * state[1 + component]
        flux.append(term + state[0] if component == axis else term)
    return flux


def acoustic_rate(state, mean_speed, halo, deriv_ref):
    flux_x = flux_along(state, mean_speed, 0)
    flux_y = flux_along(state, mean_speed, 1)
    flux_z = flux_along(state, mean_speed, 2)
    high = deriv_ref[0]
    low = deriv_ref[1]
    columns = jnp.concatenate(
        [
            jnp.concatenate([flux_x[c].reshape(64, 128), flux_y[c].reshape(64, 128)], axis=0)
            for c in range(4)
        ],
        axis=1,
    )
    column_high, column_low = split(columns)
    slopes_xy = (
        dot_nn(high[:64], column_high) + dot_nn(high[:64], column_low) + dot_nn(low[:64], column_high)
    )
    lines = jnp.concatenate([flux_z[c].reshape(64, 128) for c in range(4)], axis=0)
    line_high, line_low = split(lines)
    slopes_z = (
        dot_nn(line_high, high[64:]) + dot_nn(line_low, high[64:]) + dot_nn(line_high, low[64:])
    )
    total = [
        -(slopes_xy[:, 128 * c : 128 * c + 128] + slopes_z[64 * c : 64 * c + 64]).reshape(8, 8, 128)
        for c in range(4)
    ]
    half_lift = 0.5 * face_lift
    upwind_lift = half_lift * upwind_speed
    for side in range(2):
        plane = 0 if side == 0 else 7
        jump = [halo.face(c, 0, side) - state[c][plane] for c in range(4)]
        flux = flux_along(jump, [mean_speed[0][plane], None, None], 0)
        sign = half_lift if side == 0 else -half_lift
        for c in range(4):
            lifted = (sign * flux[c] + upwind_lift * jump[c])[None]
            zeros = jnp.zeros((7, 8, 128), F32)
            parts = [lifted, zeros] if side == 0 else [zeros, lifted]
            total[c] = total[c] + jnp.concatenate(parts, axis=0)
    for axis in (1, 2):
        position = rows((8, 8, 128)) if axis == 1 else lanes((8, 8, 128)) % 8
        is_left, is_right = position == 0, position == 7
        jump = []
        for c in range(4):
            if axis == 1:
                lower = jnp.broadcast_to(halo.face(c, 1, 0)[:, None, :], (8, 8, 128))
                upper = jnp.broadcast_to(halo.face(c, 1, 1)[:, None, :], (8, 8, 128))
            else:
                lower = halo.shifted(state[c], c, 2, 0)
                upper = halo.shifted(state[c], c, 2, 1)
            other = jnp.where(is_left, lower, jnp.where(is_right, upper, state[c]))
            jump.append(other - state[c])
        flux = flux_along(jump, mean_speed, axis)
        sign = jnp.where(is_left, half_lift, -half_lift)
        for c in range(4):
            total[c] = total[c] + (sign * flux[c] + upwind_lift * jump[c])
    return total


def pack_faces_z(planes, side):
    face = jnp.zeros((8, 128), F32)
    lane = lanes((8, 128))
    at = 0 if side == 0 else 127
    for n, plane in enumerate(planes):
        face = jnp.where(lane == n, jnp.broadcast_to(plane[:, at : at + 1], (8, 128)), face)
    return face


def quarter_transpose(groups, target):
    lane = lanes(groups[0].shape) // 32
    result = None
    for g, group in enumerate(groups):
        moved = group if g == target else pltpu.roll(group, (32 * (g - target)) % 128, 1)
        result = moved if result is None else jnp.where(lane == g, moved, result)
    return result


def projection_operands(proj_ref):
    lane = lanes((8, 128))
    row = rows((8, 128))
    tile = jnp.zeros((8, 128), F32)
    for k in range(8):
        for e in range(8):
            tile = jnp.where((row == k) & (lane % 8 == e), proj_ref[k, e], tile)
    pieces = []
    for i in range(8):
        weight = jnp.zeros((8, 128), F32)
        for a in range(8):
            weight = jnp.where(lane % 64 // 8 == a, proj_ref[i, a], weight)
        pieces.append(weight * tile)
    return tile, jnp.concatenate(pieces, axis=0)


def place_operands(tile, own_ref, slot_ref, start):
    lane = lanes((8, 128))
    row = rows((8, 128))
    block = lane // 8
    owner = jnp.zeros((8, 128), jnp.int32)
    slot = jnp.zeros((8, 128), jnp.int32)
    for b in range(16):
        owner = jnp.where(block == b, own_ref[0, 0, b], owner)
        slot = jnp.where(block == b, slot_ref[0, 0, b], slot)
    rank = jnp.zeros((8, 128), jnp.int32)
    for b in range(16):
        rank = rank + jnp.where((owner == own_ref[0, 0, b]) & (block > b), 1, 0)
    place = (owner - start) * WINDOW + rank
    columns = jnp.concatenate([jnp.where(place == n, tile, 0.0) for n in range(16)], axis=0)
    same = (lane % 8) == row
    picks = jnp.concatenate(
        [jnp.where((place == n) & same, 1.0, 0.0) for n in range(16)], axis=0
    )
    labels = dot_nt(slot.astype(F32).astype(BF16), picks.astype(BF16))
    return columns, labels


def kernel(
    sizes,
    les,
    ac,
    mf,
    proj_hbm,
    own_hbm,
    slot_hbm,
    deriv,
    les_next,
    src_v,
    ac_next,
    proj,
    own,
    slot,
    les_v,
    ac_v,
    mf_v,
    deriv_v,
    send_y,
    send_z,
    halo_x,
    halo_y,
    halo_z,
    pieces,
    arrived,
    sec_v,
    sec_send_y,
    sec_send_z,
    sec_halo_x,
    sec_halo_y,
    sec_halo_z,
    mid_v,
    mid_send_y,
    mid_send_z,
    mid_halo_x,
    mid_halo_y,
    mid_halo_z,
    rate_v,
    slope_v,
    load_sem,
    send_sem,
    recv_sem,
    piece_send,
    piece_recv,
):
    names = ("gx", "gy", "gz")
    at = [lax.axis_index(name) for name in names]
    me = at[0]
    count_x = sizes[0]

    def exists(axis, distance):
        other = at[axis] + distance
        return (other >= 0) & (other < sizes[axis])

    barrier = pltpu.get_barrier_semaphore()
    expected = jnp.int32(0)
    for axis, reach in ((0, REACH), (1, 1), (2, 1)):
        for distance in range(-reach, reach + 1):
            if distance == 0:
                continue
            near = exists(axis, distance)

            @pl.when(near)
            def _():
                pl.semaphore_signal(
                    barrier,
                    inc=1,
                    device_id={names[axis]: at[axis] + distance},
                    device_id_type=MESH,
                )

            expected = expected + jnp.where(near, 1, 0)

    loads = [
        pltpu.make_async_copy(source, target, load_sem.at[n])
        for n, (source, target) in enumerate(
            (
                (les, les_v),
                (ac, ac_v),
                (proj_hbm, proj),
                (own_hbm, own),
                (slot_hbm, slot),
                (mf, mf_v),
                (deriv, deriv_v),
            )
        )
    ]
    for load in loads:
        load.start()

    def start_of(index):
        return (index * (count_x - (WINDOW - 1))) // count_x

    start = start_of(me)

    def comes(distance):
        other = me + distance
        begin = start_of(other)
        return exists(0, distance) & (begin <= me) & (me < begin + WINDOW)

    for side, distance in ((0, -1), (1, 1)):
        for axis, refs in (
            (0, (halo_x, sec_halo_x, mid_halo_x)),
            (1, (halo_y, sec_halo_y, mid_halo_y)),
            (2, (halo_z, sec_halo_z, mid_halo_z)),
        ):

            @pl.when(jnp.logical_not(exists(axis, distance)))
            def _():
                for ref in refs:
                    ref[side] = jnp.zeros(ref.shape[1:], F32)

    for distance in range(-REACH, REACH + 1):
        if distance != 0:

            @pl.when(jnp.logical_not(comes(distance)))
            def _():
                arrived[distance + REACH] = jnp.zeros((56, 128), F32)

    def message(source, target, axis, side, slot_index):
        distance = -1 if side == 0 else 1
        return pltpu.make_async_remote_copy(
            src_ref=source,
            dst_ref=target,
            send_sem=send_sem.at[slot_index],
            recv_sem=recv_sem.at[slot_index],
            device_id={names[axis]: at[axis] + distance},
            device_id_type=MESH,
        )

    def begin(entries):
        for source, target, axis, side, slot_index in entries:

            @pl.when(exists(axis, -1 if side == 0 else 1))
            def _():
                message(source, target, axis, side, slot_index).start()

    def arrive(entries):
        for source, target, axis, side, slot_index in entries:
            @pl.when(exists(axis, 1 if side == 0 else -1))
            def _():
                message(source, target, axis, side, slot_index).wait_recv()

    def drain(entries):
        for source, target, axis, side, slot_index in entries:

            @pl.when(exists(axis, -1 if side == 0 else 1))
            def _():
                message(source, target, axis, side, slot_index).wait_send()

    flow_x = [
        (les.at[:, 0 if side == 0 else 7], halo_x.at[1 - side, 0:5], 0, side, side)
        for side in range(2)
    ]
    sound_x = [
        (ac.at[:, 0 if side == 0 else 7], halo_x.at[1 - side, 5:9], 0, side, 2 + side)
        for side in range(2)
    ]
    near_yz = [
        (send_y.at[side], halo_y.at[1 - side], 1, side, 4 + side) for side in range(2)
    ] + [(send_z.at[side], halo_z.at[1 - side], 2, side, 6 + side) for side in range(2)]
    section = (
        [
            (sec_v.at[:, 0 if side == 0 else 7], sec_halo_x.at[1 - side], 0, side, 8 + side)
            for side in range(2)
        ]
        + [
            (sec_send_y.at[side], sec_halo_y.at[1 - side], 1, side, 10 + side)
            for side in range(2)
        ]
        + [
            (sec_send_z.at[side], sec_halo_z.at[1 - side], 2, side, 12 + side)
            for side in range(2)
        ]
    )
    middle = (
        [
            (mid_v.at[:, 0 if side == 0 else 7], mid_halo_x.at[1 - side], 0, side, 14 + side)
            for side in range(2)
        ]
        + [
            (mid_send_y.at[side], mid_halo_y.at[1 - side], 1, side, 16 + side)
            for side in range(2)
        ]
        + [
            (mid_send_z.at[side], mid_halo_z.at[1 - side], 2, side, 18 + side)
            for side in range(2)
        ]
    )

    pl.semaphore_wait(barrier, expected)
    begin(flow_x)
    for load in loads[:2]:
        load.wait()
    for side in range(2):
        row = 0 if side == 0 else 7
        send_y[side, 0:5] = les_v[:, :, row, :]
        send_y[side, 5:9] = ac_v[:, :, row, :]
        send_z[side] = pack_faces_z(
            [les_v[c, x] for c in range(5) for x in range(8)]
            + [ac_v[c, x] for c in range(4) for x in range(8)],
            side,
        )

    begin(near_yz)
    begin(sound_x)
    for load in loads[2:]:
        load.wait()

    tile, plane_weights = projection_operands(proj)
    weight_high, weight_low = split(plane_weights)
    plane_operand = jnp.concatenate([weight_high, weight_low], axis=1)
    columns, labels = place_operands(tile, own, slot, start)
    column_high, column_low = split(columns)
    column_operand = jnp.concatenate(
        [
            jnp.concatenate([column_high, column_high], axis=1),
            jnp.concatenate([column_low, column_low], axis=1),
        ],
        axis=0,
    )
    for w in range(WINDOW):
        pieces[w, 48:56] = quarter_transpose([labels] * 4, w)

    state = [les_v[c] for c in range(5)]
    halo = Halo(halo_x, halo_y, halo_z, 0)
    arrive(near_yz)
    arrive(flow_x)
    lamb = lamb_vector(state, halo)
    cells = jnp.concatenate([part.reshape(64, 128) for part in lamb], axis=1)
    cell_high, cell_low = split(cells)
    stacked = jnp.concatenate([cell_high, cell_low, cell_high, cell_low], axis=0)
    planes = dot_nn(plane_operand, stacked)
    planes = jnp.concatenate([planes[:, 128 * c : 128 * c + 128] for c in range(3)], axis=0)
    plane_high, plane_low = split(planes)
    both = dot_nt(jnp.concatenate([plane_high, plane_low], axis=1), column_operand)
    placed = both[:, :128] + both[:, 128:]
    groups = [placed[48 * g : 48 * g + 48] for g in range(4)]
    for w in range(WINDOW):
        pieces[w, 0:48] = quarter_transpose(groups, w)

    def piece_copy(w):
        target = start + w
        slot_index = me - target + REACH
        return pltpu.make_async_remote_copy(
            src_ref=pieces.at[w],
            dst_ref=arrived.at[slot_index],
            send_sem=piece_send.at[w],
            recv_sem=piece_recv.at[slot_index],
            device_id={"gx": target},
            device_id_type=MESH,
        )

    for w in range(WINDOW):

        @pl.when(start + w != me)
        def _():
            piece_copy(w).start()

    arrived[REACH] = pieces[me - start]

    rate = les_rate(state, halo)
    for c in range(5):
        rate_v[c] = rate[c]
        sec_v[c] = state[c] + rate[c]
    for side in range(2):
        sec_send_y[side] = sec_v[:, :, 0 if side == 0 else 7, :]
        sec_send_z[side] = pack_faces_z(
            [sec_v[c, x] for c in range(5) for x in range(8)], side
        )
    begin(section)

    mean_speed = [mf_v[c] for c in range(3)]
    arrive(sound_x)
    sound = [ac_v[c] for c in range(4)]
    slopes = acoustic_rate(sound, mean_speed, Halo(halo_x, halo_y, halo_z, 5), deriv_v)
    for c in range(4):
        slope_v[c] = slopes[c]

    for distance in range(-REACH, REACH + 1):
        if distance != 0:

            @pl.when(comes(distance))
            def _():
                pltpu.make_async_remote_copy(
                    src_ref=pieces.at[0],
                    dst_ref=arrived.at[distance + REACH],
                    send_sem=piece_send.at[0],
                    recv_sem=piece_recv.at[distance + REACH],
                    device_id={"gx": me + distance},
                    device_id_type=MESH,
                ).wait_recv()

    halves = []
    tags = []
    zero = jnp.zeros((48, 128), F32)
    for half in range(2):
        members = [4 * half + n for n in range(4)]
        parts = [arrived[n, 0:48] if n < 7 else zero for n in members]
        quarter = [quarter_transpose(parts, g) for g in range(4)]
        halves.append(jnp.concatenate(quarter, axis=0))
        tag = jnp.zeros((8, 128), F32)
        for n in members:
            if n < 7:
                tag = jnp.where(lanes((8, 128)) // 32 == n % 4, arrived[n, 48:56], tag)
        tags.append(tag)
    same = (lanes((8, 128)) % 8) == rows((8, 128))
    picks = jnp.concatenate(
        [
            jnp.concatenate(
                [jnp.where((tag == float(s)) & same, 1.0, 0.0) for s in range(16)], axis=0
            )
            for tag in tags
        ],
        axis=1,
    ).astype(BF16)
    gathered = jnp.concatenate(halves, axis=1)
    gathered_high, gathered_low = split(gathered)
    source = dot_nt(gathered_high, picks) + dot_nt(gathered_low, picks)
    source = source.reshape(3, 8, 8, 128)
    src_v[...] = source
    for c in range(4):
        if c > 0:
            slope_v[c] = slope_v[c] + src_v[c - 1]
        mid_v[c] = ac_v[c] + acoustic_step * slope_v[c]
    for side in range(2):
        mid_send_y[side] = mid_v[:, :, 0 if side == 0 else 7, :]
        mid_send_z[side] = pack_faces_z(
            [mid_v[c, x] for c in range(4) for x in range(8)], side
        )
    begin(middle)

    arrive(section)
    rate = les_rate([sec_v[c] for c in range(5)], Halo(sec_halo_x, sec_halo_y, sec_halo_z, 0))
    for c in range(5):
        les_next[c] = les_v[c] + 0.5 * (rate_v[c] + rate[c])

    arrive(middle)
    slopes = acoustic_rate(
        [mid_v[c] for c in range(4)],
        [mf_v[c] for c in range(3)],
        Halo(mid_halo_x, mid_halo_y, mid_halo_z, 0),
        deriv_v,
    )
    for c in range(4):
        total = slope_v[c] + slopes[c]
        if c > 0:
            total = total + src_v[c - 1]
        ac_next[c] = ac_v[c] + 0.5 * acoustic_step * total

    drain(flow_x)
    drain(sound_x)
    drain(near_yz)
    drain(section)
    drain(middle)
    for w in range(WINDOW):

        @pl.when(start + w != me)
        def _():
            piece_copy(w).wait_send()


def write_out(les_v, src_v, ac_v, les_out, src_out, ac_out, sems):
    copies = [
        pltpu.make_async_copy(source, target, sems.at[n])
        for n, (source, target) in enumerate(((les_v, les_out), (src_v, src_out), (ac_v, ac_out)))
    ]
    for copy in copies:
        copy.start()
    for copy in copies:
        copy.wait()


def local(les_state, acoustic_state, mean_flow, projection, target_owner, target_slot):
    sizes = tuple(lax.axis_size(name) for name in ("gx", "gy", "gz"))
    deriv = jnp.asarray(derivative_operands())
    anywhere = pl.BlockSpec(memory_space=pl.ANY)
    scalars = pl.BlockSpec(memory_space=pltpu.SMEM)

    def vmem(*shape):
        return pltpu.VMEM(shape, F32)

    def halos(n):
        return [vmem(2, n, 8, 128), vmem(2, n, 8, 128), vmem(2, 8, 128)]

    field = (8, 8, 128)
    shapes = [(5,) + field, (3,) + field, (4,) + field]
    on_chip = pl.BlockSpec(memory_space=pltpu.VMEM)
    results = pl.pallas_call(
        functools.partial(kernel, sizes),
        name="coupled_step",
        out_shape=tuple(pltpu.VMEM(shape, F32) for shape in shapes),
        in_specs=[anywhere] * 7,
        out_specs=(on_chip,) * 3,
        scratch_shapes=[
            pltpu.SMEM((8, 8), F32),
            pltpu.SMEM((1, 1, 16), jnp.int32),
            pltpu.SMEM((1, 1, 16), jnp.int32),
            vmem(5, *field),
            vmem(4, *field),
            vmem(3, *field),
            pltpu.VMEM((2, 192, 128), BF16),
            vmem(2, 9, 8, 128),
            vmem(2, 8, 128),
            *halos(9),
            vmem(4, 56, 128),
            vmem(7, 56, 128),
            vmem(5, *field),
            vmem(2, 5, 8, 128),
            vmem(2, 8, 128),
            *halos(5),
            vmem(4, *field),
            vmem(2, 4, 8, 128),
            vmem(2, 8, 128),
            *halos(4),
            vmem(5, *field),
            vmem(4, *field),
            pltpu.SemaphoreType.DMA((7,)),
            pltpu.SemaphoreType.DMA((20,)),
            pltpu.SemaphoreType.DMA((20,)),
            pltpu.SemaphoreType.DMA((4,)),
            pltpu.SemaphoreType.DMA((7,)),
        ],
        compiler_params=pltpu.CompilerParams(collective_id=0, has_side_effects=True),
    )(les_state, acoustic_state, mean_flow, projection, target_owner, target_slot, deriv)
    return pl.pallas_call(
        write_out,
        name="write_out",
        out_shape=tuple(jax.ShapeDtypeStruct(shape, F32) for shape in shapes),
        in_specs=[on_chip] * 3,
        out_specs=(anywhere,) * 3,
        scratch_shapes=[pltpu.SemaphoreType.DMA((3,))],
    )(*[pltpu.with_memory_space_constraint(result, pltpu.VMEM) for result in results])


def solution(mesh):
    fields = P(None, "gx", "gy", "gz")
    blocks = P("gx", "gy", "gz")
    return jax.shard_map(
        local,
        mesh=mesh,
        in_specs=(fields, fields, fields, P(), blocks, blocks),
        out_specs=(fields, fields, fields),
        check_vma=False,
    )
```

```python
import functools

import jax
import jax.numpy as jnp
import numpy as np
from jax import lax
from jax.experimental import pallas as pl
from jax.experimental.pallas import tpu as pltpu
from jax.sharding import PartitionSpec as P

MESH = pl.DeviceIdType.MESH
F32 = jnp.float32
BF16 = jnp.bfloat16

lobatto_points = np.array(
    [
        -1.0,
        -0.8717401485096066,
        -0.5917001814331423,
        -0.2092992179024789,
        0.2092992179024789,
        0.5917001814331423,
        0.8717401485096066,
        1.0,
    ]
)
flux_half = 0.08
gamma_less = 0.4
acoustic_step = 0.01
upwind_speed = 1.5
face_lift = 28.0
REACH = 4
ROWS = 64
WINDOW = 4


def derivative_matrix():
    points = lobatto_points
    gaps = points[:, None] - points[None, :] + np.eye(8)
    products = np.prod(gaps, axis=1)
    matrix = products[:, None] / (products[None, :] * gaps)
    np.fill_diagonal(matrix, 0.0)
    np.fill_diagonal(matrix, -matrix.sum(axis=1))
    return matrix


def derivative_operands():
    deriv = derivative_matrix()
    eye = np.eye(8)
    along_xy = np.concatenate([np.kron(deriv, eye), np.kron(eye, deriv)], axis=1)
    along_z = np.kron(np.eye(16), deriv.T)
    whole = np.concatenate([along_xy, along_z], axis=0).astype(np.float32)
    high = whole.astype(jnp.bfloat16)
    low = (whole - high.astype(np.float32)).astype(jnp.bfloat16)
    return np.stack([high, low])


def split(value):
    high = value.astype(BF16)
    return high, (value - high.astype(F32)).astype(BF16)


def dot_nn(left, right):
    return lax.dot_general(left, right, (((1,), (0,)), ((), ())), preferred_element_type=F32)


def dot_nt(left, right):
    return lax.dot_general(left, right, (((1,), (1,)), ((), ())), preferred_element_type=F32)


def lanes(shape):
    return lax.broadcasted_iota(jnp.int32, shape, len(shape) - 1)


def rows(shape):
    return lax.broadcasted_iota(jnp.int32, shape, len(shape) - 2)


class Halo:
    def __init__(self, x_ref, y_ref, z_ref, first):
        self.x_ref, self.y_ref, self.z_ref, self.first = x_ref, y_ref, z_ref, first

    def face(self, component, axis, side):
        at = self.first + component
        if axis == 0:
            return self.x_ref[side, at]
        if axis == 1:
            return self.y_ref[side, at]
        face = self.z_ref[side]
        return [jnp.broadcast_to(face[:, 8 * at + x : 8 * at + x + 1], (8, 128)) for x in range(8)]

    def shifted(self, field, component, axis, side):
        return shift(field, self.face(component, axis, side), axis, side)


def shift(field, face, axis, side):
    if axis == 0:
        if side == 0:
            return jnp.concatenate([face[None], field[:-1]], axis=0)
        return jnp.concatenate([field[1:], face[None]], axis=0)
    if axis == 1:
        rolled = pltpu.roll(field, 1 if side == 0 else 7, 1)
        edge = rows((8, 8, 128)) == (0 if side == 0 else 7)
        return jnp.where(edge, jnp.broadcast_to(face[:, None, :], (8, 8, 128)), rolled)
    rolled = pltpu.roll(field, 1 if side == 0 else 127, 2)
    edge = lanes((8, 8, 128)) == (0 if side == 0 else 127)
    return jnp.where(edge, jnp.stack(face), rolled)


def les_rate(state, halo):
    total = [-6.0 * part for part in state]
    for axis in range(3):
        for side in range(2):
            near = [halo.shifted(state[c], c, axis, side) for c in range(5)]
            momentum = near[1:4]
            energy = near[4] + 2.5
            inverse = 1.0 / (near[0] + 1.0)
            square = (
                momentum[0] * momentum[0] + momentum[1] * momentum[1] + momentum[2] * momentum[2]
            )
            pressure = gamma_less * (energy - 0.5 * (square * inverse))
            speed = momentum[axis] * inverse
            flux = [momentum[axis]]
            for component in range(3):
                term = momentum[component] * speed
                flux.append(term + pressure if component == axis else term)
            flux.append((energy + pressure) * speed)
            for c in range(5):
                total[c] = total[c] + (near[c] + flux[c] if side == 0 else near[c] - flux[c])
    return [flux_half * part for part in total]


def lamb_vector(state, halo):
    inverse = 1.0 / (state[0] + 1.0)
    velocity = [state[1 + c] * inverse for c in range(3)]
    packed = []
    for side in range(2):
        face = halo.z_ref[side]
        inverse_face = 1.0 / (face + 1.0)
        packed.append([face * pltpu.roll(inverse_face, 8 * (1 + c), 1) for c in range(3)])

    def near(component, axis, side):
        if axis == 2:
            face = packed[side][component]
            start = 8 * (1 + component)
            face = [jnp.broadcast_to(face[:, start + x : start + x + 1], (8, 128)) for x in range(8)]
        else:
            face = halo.face(1 + component, axis, side) / (halo.face(0, axis, side) + 1.0)
        return shift(velocity[component], face, axis, side)

    def slope(component, axis):
        return 0.5 * (near(component, axis, 1) - near(component, axis, 0))

    vort_x = slope(2, 1) - slope(1, 2)
    vort_y = slope(0, 2) - slope(2, 0)
    vort_z = slope(1, 0) - slope(0, 1)
    return [
        vort_y * velocity[2] - vort_z * velocity[1],
        vort_z * velocity[0] - vort_x * velocity[2],
        vort_x * velocity[1] - vort_y * velocity[0],
    ]


def flux_along(state, mean_speed, axis):
    flux = [mean_speed[axis] * state[0] + state[1 + axis]]
    for component in range(3):
        term = mean_speed[axis] * state[1 + component]
        flux.append(term + state[0] if component == axis else term)
    return flux


def acoustic_rate(state, mean_speed, halo, deriv_ref):
    flux_x = flux_along(state, mean_speed, 0)
    flux_y = flux_along(state, mean_speed, 1)
    flux_z = flux_along(state, mean_speed, 2)
    high = deriv_ref[0]
    low = deriv_ref[1]
    columns = jnp.concatenate(
        [
            jnp.concatenate([flux_x[c].reshape(64, 128), flux_y[c].reshape(64, 128)], axis=0)
            for c in range(4)
        ],
        axis=1,
    )
    column_high, column_low = split(columns)
    slopes_xy = (
        dot_nn(high[:64], column_high) + dot_nn(high[:64], column_low) + dot_nn(low[:64], column_high)
    )
    lines = jnp.concatenate([flux_z[c].reshape(64, 128) for c in range(4)], axis=0)
    line_high, line_low = split(lines)
    slopes_z = (
        dot_nn(line_high, high[64:]) + dot_nn(line_low, high[64:]) + dot_nn(line_high, low[64:])
    )
    total = [
        -(slopes_xy[:, 128 * c : 128 * c + 128] + slopes_z[64 * c : 64 * c + 64]).reshape(8, 8, 128)
        for c in range(4)
    ]
    half_lift = 0.5 * face_lift
    upwind_lift = half_lift * upwind_speed
    for side in range(2):
        plane = 0 if side == 0 else 7
        jump = [halo.face(c, 0, side) - state[c][plane] for c in range(4)]
        flux = flux_along(jump, [mean_speed[0][plane], None, None], 0)
        sign = half_lift if side == 0 else -half_lift
        for c in range(4):
            lifted = (sign * flux[c] + upwind_lift * jump[c])[None]
            zeros = jnp.zeros((7, 8, 128), F32)
            parts = [lifted, zeros] if side == 0 else [zeros, lifted]
            total[c] = total[c] + jnp.concatenate(parts, axis=0)
    for axis in (1, 2):
        position = rows((8, 8, 128)) if axis == 1 else lanes((8, 8, 128)) % 8
        is_left, is_right = position == 0, position == 7
        jump = []
        for c in range(4):
            if axis == 1:
                lower = jnp.broadcast_to(halo.face(c, 1, 0)[:, None, :], (8, 8, 128))
                upper = jnp.broadcast_to(halo.face(c, 1, 1)[:, None, :], (8, 8, 128))
            else:
                lower = halo.shifted(state[c], c, 2, 0)
                upper = halo.shifted(state[c], c, 2, 1)
            other = jnp.where(is_left, lower, jnp.where(is_right, upper, state[c]))
            jump.append(other - state[c])
        flux = flux_along(jump, mean_speed, axis)
        sign = jnp.where(is_left, half_lift, -half_lift)
        for c in range(4):
            total[c] = total[c] + (sign * flux[c] + upwind_lift * jump[c])
    return total


def pack_faces_z(planes, side):
    return pack_lane(planes, 127 * side, 0)


def pack_lane(planes, at, first):
    face = jnp.zeros((8, 128), F32)
    lane = lanes((8, 128))
    for n, plane in enumerate(planes, first):
        face = jnp.where(lane == n, jnp.broadcast_to(plane[:, at : at + 1], (8, 128)), face)
    return face


def quarter_transpose(groups, target):
    lane = lanes(groups[0].shape) // 32
    result = None
    for g, group in enumerate(groups):
        moved = group if g == target else pltpu.roll(group, (32 * (g - target)) % 128, 1)
        result = moved if result is None else jnp.where(lane == g, moved, result)
    return result


def projection_operands(proj_ref):
    lane = lanes((8, 128))
    row = rows((8, 128))
    tile = jnp.zeros((8, 128), F32)
    for k in range(8):
        for e in range(8):
            tile = jnp.where((row == k) & (lane % 8 == e), proj_ref[k, e], tile)
    pieces = []
    for i in range(8):
        weight = jnp.zeros((8, 128), F32)
        for a in range(8):
            weight = jnp.where(lane % 64 // 8 == a, proj_ref[i, a], weight)
        pieces.append(weight * tile)
    return tile, jnp.concatenate(pieces, axis=0)


def place_operands(tile, own_ref, slot_ref, start):
    lane = lanes((8, 128))
    row = rows((8, 128))
    block = lane // 8
    owner = jnp.zeros((8, 128), jnp.int32)
    slot = jnp.zeros((8, 128), jnp.int32)
    for b in range(16):
        owner = jnp.where(block == b, own_ref[0, 0, b], owner)
        slot = jnp.where(block == b, slot_ref[0, 0, b], slot)
    rank = jnp.zeros((8, 128), jnp.int32)
    for b in range(16):
        rank = rank + jnp.where((owner == own_ref[0, 0, b]) & (block > b), 1, 0)
    place = (owner - start) * WINDOW + rank
    columns = jnp.concatenate([jnp.where(place == n, tile, 0.0) for n in range(16)], axis=0)
    same = (lane % 8) == row
    picks = jnp.concatenate(
        [jnp.where((place == n) & same, 1.0, 0.0) for n in range(16)], axis=0
    )
    labels = dot_nt(slot.astype(F32).astype(BF16), picks.astype(BF16))
    return columns, labels


def kernel(
    sizes,
    les,
    ac,
    mf,
    proj_hbm,
    own_hbm,
    slot_hbm,
    deriv,
    les_next,
    src_v,
    ac_next,
    proj,
    own,
    slot,
    les_v,
    ac_v,
    mf_v,
    deriv_v,
    send_y,
    send_z,
    halo_x,
    halo_y,
    halo_z,
    pieces,
    arrived,
    sec_v,
    sec_send_y,
    sec_send_z,
    sec_halo_x,
    sec_halo_y,
    sec_halo_z,
    mid_v,
    mid_send_y,
    mid_send_z,
    mid_halo_x,
    mid_halo_y,
    mid_halo_z,
    placed_v,
    side_tiles,
    side_arrived,
    end_rows,
    end_arrived,
    rate_v,
    slope_v,
    load_sem,
    send_sem,
    recv_sem,
    piece_send,
    piece_recv,
    side_send,
    side_recv,
):
    names = ("gx", "gy", "gz")
    at = [lax.axis_index(name) for name in names]
    me = at[0]
    count_x = sizes[0]

    def exists(axis, distance):
        other = at[axis] + distance
        return (other >= 0) & (other < sizes[axis])

    barrier = pltpu.get_barrier_semaphore()
    expected = jnp.int32(0)
    for axis, reach in ((0, REACH), (1, 1), (2, 1)):
        for distance in range(-reach, reach + 1):
            if distance == 0:
                continue
            near = exists(axis, distance)

            @pl.when(near)
            def _():
                pl.semaphore_signal(
                    barrier,
                    inc=1,
                    device_id={names[axis]: at[axis] + distance},
                    device_id_type=MESH,
                )

            expected = expected + jnp.where(near, 1, 0)

    loads = [
        pltpu.make_async_copy(source, target, load_sem.at[n])
        for n, (source, target) in enumerate(
            (
                (les, les_v),
                (ac, ac_v),
                (proj_hbm, proj),
                (own_hbm, own),
                (slot_hbm, slot),
                (mf, mf_v),
                (deriv, deriv_v),
            )
        )
    ]
    for load in loads:
        load.start()

    def start_of(index):
        return (index * (count_x - (WINDOW - 1))) // count_x

    start = start_of(me)

    def comes(distance):
        other = me + distance
        begin = start_of(other)
        return exists(0, distance) & (begin <= me) & (me < begin + WINDOW)

    def grazes(distance):
        begin = start_of(me + distance)
        return exists(0, distance) & ((me + 1 == begin) | (me == begin + WINDOW))

    for side, distance in ((0, -1), (1, 1)):
        for axis, refs in (
            (0, (halo_x, sec_halo_x, mid_halo_x)),
            (1, (halo_y, sec_halo_y, mid_halo_y)),
            (2, (halo_z, sec_halo_z, mid_halo_z)),
        ):

            @pl.when(jnp.logical_not(exists(axis, distance)))
            def _():
                for ref in refs:
                    ref[side] = jnp.zeros(ref.shape[1:], F32)

    for distance in range(-REACH, REACH + 1):
        if distance != 0:

            grazed, other = (56, 48) if distance > 0 else (48, 56)

            @pl.when(jnp.logical_not(comes(distance)))
            def _():
                arrived[distance + REACH, 0:48] = jnp.zeros((48, 128), F32)
                arrived[distance + REACH, other : other + 8] = jnp.zeros((8, 128), F32)

            @pl.when(jnp.logical_not(comes(distance) | grazes(distance)))
            def _():
                arrived[distance + REACH, grazed : grazed + 8] = jnp.zeros((8, 128), F32)

    def side_of(n):
        return 1 + n // 2, 2 * (n % 2) - 1

    def side_comes(n, distance):
        return exists(*side_of(n)) & comes(distance)

    for n in range(4):
        for distance in range(-3, 4):

            @pl.when(jnp.logical_not(side_comes(n, distance)))
            def _():
                if n < 2:
                    side_arrived[n, distance + 3] = jnp.zeros((8, 128), F32)
                else:
                    end_arrived[n - 2, distance + 3] = jnp.zeros((1, 256), F32)

    def message(source, target, axis, side, slot_index):
        distance = -1 if side == 0 else 1
        return pltpu.make_async_remote_copy(
            src_ref=source,
            dst_ref=target,
            send_sem=send_sem.at[slot_index],
            recv_sem=recv_sem.at[slot_index],
            device_id={names[axis]: at[axis] + distance},
            device_id_type=MESH,
        )

    def begin(entries):
        for source, target, axis, side, slot_index in entries:

            @pl.when(exists(axis, -1 if side == 0 else 1))
            def _():
                message(source, target, axis, side, slot_index).start()

    def arrive(entries):
        for source, target, axis, side, slot_index in entries:
            @pl.when(exists(axis, 1 if side == 0 else -1))
            def _():
                message(source, target, axis, side, slot_index).wait_recv()

    def drain(entries):
        for source, target, axis, side, slot_index in entries:

            @pl.when(exists(axis, -1 if side == 0 else 1))
            def _():
                message(source, target, axis, side, slot_index).wait_send()

    flow_x = [
        (les.at[:, 0 if side == 0 else 7], halo_x.at[1 - side, 0:5], 0, side, side)
        for side in range(2)
    ]
    flow_y = [
        (send_y.at[side, 0:5], halo_y.at[1 - side, 0:5], 1, side, 4 + side) for side in range(2)
    ]
    both_z = [(send_z.at[side], halo_z.at[1 - side], 2, side, 6 + side) for side in range(2)]
    sound = [
        (ac.at[:, 0 if side == 0 else 7], halo_x.at[1 - side, 5:9], 0, side, 2 + side)
        for side in range(2)
    ] + [
        (send_y.at[side, 5:9], halo_y.at[1 - side, 5:9], 1, side, 20 + side) for side in range(2)
    ]
    section = (
        [
            (sec_v.at[:, 0 if side == 0 else 7], sec_halo_x.at[1 - side], 0, side, 8 + side)
            for side in range(2)
        ]
        + [
            (sec_send_y.at[side], sec_halo_y.at[1 - side], 1, side, 10 + side)
            for side in range(2)
        ]
        + [
            (sec_send_z.at[side], sec_halo_z.at[1 - side], 2, side, 12 + side)
            for side in range(2)
        ]
    )
    middle = (
        [
            (mid_v.at[:, 0 if side == 0 else 7], mid_halo_x.at[1 - side], 0, side, 14 + side)
            for side in range(2)
        ]
        + [
            (mid_send_y.at[side], mid_halo_y.at[1 - side], 1, side, 16 + side)
            for side in range(2)
        ]
        + [
            (mid_send_z.at[side], mid_halo_z.at[1 - side], 2, side, 18 + side)
            for side in range(2)
        ]
    )

    pl.semaphore_wait(barrier, expected)
    begin(flow_x)
    for load in loads[:2]:
        load.wait()
    for side in range(2):
        row = 0 if side == 0 else 7
        send_y[side, 0:5] = les_v[:, :, row, :]
        send_y[side, 5:9] = ac_v[:, :, row, :]
        send_z[side] = pack_faces_z(
            [les_v[c, x] for c in range(5) for x in range(8)]
            + [ac_v[c, x] for c in range(4) for x in range(8)],
            side,
        )

    begin(flow_y)
    begin(both_z)
    begin(sound)
    for load in loads[2:]:
        load.wait()

    tile, plane_weights = projection_operands(proj)
    weight_high, weight_low = split(plane_weights)
    plane_operand = jnp.concatenate([weight_high, weight_low], axis=1)
    columns, labels = place_operands(tile, own, slot, start)
    column_high, column_low = split(columns)
    column_operand = jnp.concatenate(
        [
            jnp.concatenate([column_high, column_high], axis=1),
            jnp.concatenate([column_low, column_low], axis=1),
        ],
        axis=0,
    )
    state = [les_v[c] for c in range(5)]
    halo = Halo(halo_x, halo_y, halo_z, 0)
    arrive(flow_y)
    arrive(both_z)
    arrive(flow_x)
    lamb = lamb_vector(state, halo)
    cells = jnp.concatenate([part.reshape(64, 128) for part in lamb], axis=1)
    cell_high, cell_low = split(cells)
    stacked = jnp.concatenate([cell_high, cell_low, cell_high, cell_low], axis=0)
    planes = dot_nn(plane_operand, stacked)
    planes = jnp.concatenate([planes[:, 128 * c : 128 * c + 128] for c in range(3)], axis=0)
    plane_high, plane_low = split(planes)
    both = dot_nt(jnp.concatenate([plane_high, plane_low], axis=1), column_operand)
    placed = both[:, :128] + both[:, 128:]
    groups = [placed[48 * g : 48 * g + 48] for g in range(4)]
    lows = [placed[64 * c : 64 * c + 8] for c in range(3)] + [labels]
    highs = [placed[64 * c + 56 : 64 * c + 64] for c in range(3)] + [labels]
    for w in range(WINDOW):
        pieces[w + 1, 0:48] = quarter_transpose(groups, w)
    lane = lanes((8, 128))
    row = rows((8, 128))
    for w in range(-1, WINDOW + 1):
        zero = jnp.zeros((8, 128), F32)
        above = quarter_transpose(highs, w - 1) if w >= 1 else zero
        below = quarter_transpose(lows, w + 1) if w + 1 < WINDOW else zero
        if 0 <= w < WINDOW:
            moved = labels if w == 3 else pltpu.roll(labels, 32 * (3 - w), 1)
            above = jnp.where((lane >= 96) & (row >= 4), moved, above)
        pieces[w + 1, 48:56] = above
        pieces[w + 1, 56:64] = below

    def piece_copy(w):
        target = start + w
        slot_index = me - target + REACH
        return pltpu.make_async_remote_copy(
            src_ref=pieces.at[w + 1],
            dst_ref=arrived.at[slot_index],
            send_sem=piece_send.at[w + 1],
            recv_sem=piece_recv.at[slot_index],
            device_id={"gx": target},
            device_id_type=MESH,
        )

    def edge_copy(w):
        target = start + w
        slot_index = me - target + REACH
        part = slice(56, 64) if w < 0 else slice(48, 56)
        return pltpu.make_async_remote_copy(
            src_ref=pieces.at[w + 1, part],
            dst_ref=arrived.at[slot_index, part],
            send_sem=piece_send.at[w + 1],
            recv_sem=piece_recv.at[slot_index],
            device_id={"gx": target},
            device_id_type=MESH,
        )

    for w in range(WINDOW):

        @pl.when(start + w != me)
        def _():
            piece_copy(w).start()

    @pl.when(start >= 1)
    def _():
        edge_copy(-1).start()

    @pl.when(start + WINDOW < count_x)
    def _():
        edge_copy(WINDOW).start()

    arrived[REACH] = pieces[me - start + 1]

    def side_copy(n, w):
        axis, distance = side_of(n)
        target = start + w
        slot_index = me - target + 3
        landing = n + 1 - 2 * (n % 2)
        if n < 2:
            source, goal = side_tiles.at[n, w], side_arrived.at[landing, slot_index]
        else:
            source, goal = end_rows.at[4 * (n - 2) + w], end_arrived.at[landing - 2, slot_index]
        return pltpu.make_async_remote_copy(
            src_ref=source,
            dst_ref=goal,
            send_sem=side_send.at[4 * n + w],
            recv_sem=side_recv.at[7 * landing + slot_index],
            device_id={"gx": target, names[axis]: at[axis] + distance},
            device_id_type=MESH,
        )

    def side_begin(n):
        @pl.when(exists(*side_of(n)))
        def _():
            for w in range(WINDOW):
                side_copy(n, w).start()

    placed_v[...] = placed.reshape(3, 8, 8, 128)
    for n in range(2):
        parts = [placed_v[c, :, 7 * n, :] for c in range(3)] + [labels]
        for w in range(WINDOW):
            side_tiles[n, w] = quarter_transpose(parts, w)
        side_begin(n)
    upper = row >= 4
    wanted = (
        (lane // 32 == row % 4)
        & (lane % 8 == jnp.where(upper, 7, 0))
        & (labels == jnp.where(upper, 15.0, 0.0))
    )
    ends = jnp.where(wanted, 1.0, 0.0).astype(BF16)
    placed_high, placed_low = split(
        jnp.concatenate([placed, jnp.zeros((64, 128), F32)], axis=0)
    )
    sums = dot_nt(ends, placed_high) + dot_nt(ends, placed_low)
    for n in range(8):
        end_rows[n] = sums[n : n + 1]
    side_begin(2)
    side_begin(3)

    rate = les_rate(state, halo)
    for c in range(5):
        rate_v[c] = rate[c]
        sec_v[c] = state[c] + rate[c]
    for side in range(2):
        sec_send_y[side] = sec_v[:, :, 0 if side == 0 else 7, :]
        sec_send_z[side] = pack_faces_z(
            [sec_v[c, x] for c in range(5) for x in range(8)], side
        )
    begin(section)

    mean_speed = [mf_v[c] for c in range(3)]
    arrive(sound)
    slopes = acoustic_rate(
        [ac_v[c] for c in range(4)], mean_speed, Halo(halo_x, halo_y, halo_z, 5), deriv_v
    )
    for c in range(4):
        slope_v[c] = slopes[c]
        mid_v[c] = ac_v[c] + acoustic_step * slopes[c]
    for side in range(2):
        mid_send_y[side] = mid_v[:, :, 0 if side == 0 else 7, :]
        mid_send_z[side] = pack_faces_z([mid_v[c, x] for c in range(4) for x in range(8)], side)
    begin(middle)

    for distance in range(-REACH, REACH + 1):
        if distance != 0:

            @pl.when(comes(distance))
            def _():
                pltpu.make_async_remote_copy(
                    src_ref=pieces.at[0],
                    dst_ref=arrived.at[distance + REACH],
                    send_sem=piece_send.at[0],
                    recv_sem=piece_recv.at[distance + REACH],
                    device_id={"gx": me + distance},
                    device_id_type=MESH,
                ).wait_recv()

            @pl.when(grazes(distance))
            def _():
                part = slice(56, 64) if distance > 0 else slice(48, 56)
                pltpu.make_async_remote_copy(
                    src_ref=pieces.at[0, part],
                    dst_ref=arrived.at[distance + REACH, part],
                    send_sem=piece_send.at[0],
                    recv_sem=piece_recv.at[distance + REACH],
                    device_id={"gx": me + distance},
                    device_id_type=MESH,
                ).wait_recv()

    for n in range(4):
        for distance in range(-3, 4):

            @pl.when(side_comes(n, distance))
            def _():
                axis, step = side_of(n)
                if n < 2:
                    source, goal = side_tiles.at[0, 0], side_arrived.at[n, distance + 3]
                else:
                    source, goal = end_rows.at[0], end_arrived.at[n - 2, distance + 3]
                pltpu.make_async_remote_copy(
                    src_ref=source,
                    dst_ref=goal,
                    send_sem=side_send.at[0],
                    recv_sem=side_recv.at[7 * n + distance + 3],
                    device_id={"gx": me + distance, names[axis]: at[axis] + step},
                    device_id_type=MESH,
                ).wait_recv()

    same = (lanes((8, 128)) % 8) == rows((8, 128))

    def picks_of(tags):
        return jnp.concatenate(
            [
                jnp.concatenate(
                    [jnp.where((tag == float(n)) & same, 1.0, 0.0) for n in range(16)], axis=0
                )
                for tag in tags
            ],
            axis=1,
        ).astype(BF16)

    def gather(halves, tags):
        picks = picks_of(tags)
        high, low = split(jnp.concatenate(halves, axis=1))
        return dot_nt(high, picks) + dot_nt(low, picks)

    def members_of(half, first, part):
        members = [first + REACH + 4 * half + n for n in range(4)]
        zero = jnp.zeros((part.stop - part.start, 128), F32)
        return [arrived[n, part] if 4 * half + k < 7 else zero for k, n in enumerate(members)]

    halves, tags = [], []
    for half in range(2):
        parts = members_of(half, -3, slice(0, 48))
        halves.append(
            jnp.concatenate([quarter_transpose(parts, g) for g in range(4)], axis=0)
        )
        tag = quarter_transpose(members_of(half, -3, slice(48, 56)), 3)
        tags.append(jnp.broadcast_to(tag[4:5], (8, 128)))
    src_v[...] = gather(halves, tags).reshape(3, 8, 8, 128)

    def gather_tiles(tiles):
        halves, tags = [], []
        for parts in (tiles[:4], tiles[4:] + [jnp.zeros((8, 128), F32)]):
            halves.append(
                jnp.concatenate([quarter_transpose(parts, c) for c in range(3)], axis=0)
            )
            tag = quarter_transpose(parts, 3)
            tags.append(jnp.broadcast_to(tag[0:1], (8, 128)))
        return gather(halves, tags)

    source_x = [
        gather_tiles([arrived[first + n, part] for n in range(7)])
        for first, part in ((0, slice(48, 56)), (2, slice(56, 64)))
    ]
    line = lax.broadcasted_iota(jnp.int32, (256, 128), 0)
    folds = jnp.where(lanes((256, 128)) == 8 + line // 8, 1.0, 0.0).astype(BF16)
    source_z = []
    for side in range(2):
        line_sum = end_arrived[side, 0]
        for n in range(1, 7):
            line_sum = line_sum + end_arrived[side, n]
        spread = jnp.broadcast_to(line_sum, (8, 256))
        spread = jnp.where(lanes((8, 256)) % 8 == rows((8, 256)), spread, 0.0)
        spread_high, spread_low = split(spread)
        source_z.append(dot_nn(spread_high, folds) + dot_nn(spread_low, folds))
    source_y = [gather_tiles([side_arrived[side, n] for n in range(7)]) for side in range(2)]

    arrive(section)
    rate = les_rate([sec_v[c] for c in range(5)], Halo(sec_halo_x, sec_halo_y, sec_halo_z, 0))
    for c in range(5):
        les_next[c] = les_v[c] + 0.5 * (rate_v[c] + rate[c])

    arrive(middle)
    for side in range(2):
        mid_halo_z[side] = mid_halo_z[side] + acoustic_step * source_z[side]
        for c in range(3):
            for ref, face in ((mid_halo_x, source_x[side]), (mid_halo_y, source_y[side])):
                ref[side, 1 + c] = ref[side, 1 + c] + acoustic_step * face[8 * c : 8 * c + 8]
    slopes = acoustic_rate(
        [mid_v[0]] + [mid_v[1 + c] + acoustic_step * src_v[c] for c in range(3)],
        mean_speed,
        Halo(mid_halo_x, mid_halo_y, mid_halo_z, 0),
        deriv_v,
    )
    for c in range(4):
        total = slope_v[c] + slopes[c]
        if c > 0:
            total = total + 2.0 * src_v[c - 1]
        ac_next[c] = ac_v[c] + 0.5 * acoustic_step * total

    drain(flow_x)
    drain(flow_y)
    drain(both_z)
    drain(sound)
    drain(section)
    drain(middle)

    for n in range(4):

        @pl.when(exists(*side_of(n)))
        def _():
            for w in range(WINDOW):
                side_copy(n, w).wait_send()

    @pl.when(start >= 1)
    def _():
        edge_copy(-1).wait_send()

    @pl.when(start + WINDOW < count_x)
    def _():
        edge_copy(WINDOW).wait_send()

    for w in range(WINDOW):

        @pl.when(start + w != me)
        def _():
            piece_copy(w).wait_send()


def write_out(les_v, src_v, ac_v, les_out, src_out, ac_out, sems):
    copies = [
        pltpu.make_async_copy(source, target, sems.at[n])
        for n, (source, target) in enumerate(((les_v, les_out), (src_v, src_out), (ac_v, ac_out)))
    ]
    for copy in copies:
        copy.start()
    for copy in copies:
        copy.wait()


def local(les_state, acoustic_state, mean_flow, projection, target_owner, target_slot):
    sizes = tuple(lax.axis_size(name) for name in ("gx", "gy", "gz"))
    deriv = jnp.asarray(derivative_operands())
    anywhere = pl.BlockSpec(memory_space=pl.ANY)
    scalars = pl.BlockSpec(memory_space=pltpu.SMEM)

    def vmem(*shape):
        return pltpu.VMEM(shape, F32)

    def halos(n):
        return [vmem(2, n, 8, 128), vmem(2, n, 8, 128), vmem(2, 8, 128)]

    field = (8, 8, 128)
    shapes = [(5,) + field, (3,) + field, (4,) + field]
    on_chip = pl.BlockSpec(memory_space=pltpu.VMEM)
    results = pl.pallas_call(
        functools.partial(kernel, sizes),
        name="coupled_step",
        out_shape=tuple(pltpu.VMEM(shape, F32) for shape in shapes),
        in_specs=[anywhere] * 7,
        out_specs=(on_chip,) * 3,
        scratch_shapes=[
            pltpu.SMEM((8, 8), F32),
            pltpu.SMEM((1, 1, 16), jnp.int32),
            pltpu.SMEM((1, 1, 16), jnp.int32),
            vmem(5, *field),
            vmem(4, *field),
            vmem(3, *field),
            pltpu.VMEM((2, 192, 128), BF16),
            vmem(2, 9, 8, 128),
            vmem(2, 8, 128),
            *halos(9),
            vmem(6, ROWS, 128),
            vmem(9, ROWS, 128),
            vmem(5, *field),
            vmem(2, 5, 8, 128),
            vmem(2, 8, 128),
            *halos(5),
            vmem(4, *field),
            vmem(2, 4, 8, 128),
            vmem(2, 8, 128),
            *halos(4),
            vmem(3, *field),
            vmem(2, 4, 8, 128),
            vmem(2, 7, 8, 128),
            vmem(8, 1, 256),
            vmem(2, 7, 1, 256),
            vmem(5, *field),
            vmem(4, *field),
            pltpu.SemaphoreType.DMA((7,)),
            pltpu.SemaphoreType.DMA((22,)),
            pltpu.SemaphoreType.DMA((22,)),
            pltpu.SemaphoreType.DMA((6,)),
            pltpu.SemaphoreType.DMA((9,)),
            pltpu.SemaphoreType.DMA((16,)),
            pltpu.SemaphoreType.DMA((28,)),
        ],
        compiler_params=pltpu.CompilerParams(collective_id=0, has_side_effects=True),
    )(les_state, acoustic_state, mean_flow, projection, target_owner, target_slot, deriv)
    return pl.pallas_call(
        write_out,
        name="write_out",
        out_shape=tuple(jax.ShapeDtypeStruct(shape, F32) for shape in shapes),
        in_specs=[on_chip] * 3,
        out_specs=(anywhere,) * 3,
        scratch_shapes=[pltpu.SemaphoreType.DMA((3,))],
    )(*[pltpu.with_memory_space_constraint(result, pltpu.VMEM) for result in results])


def solution(mesh):
    fields = P(None, "gx", "gy", "gz")
    blocks = P("gx", "gy", "gz")
    return jax.shard_map(
        local,
        mesh=mesh,
        in_specs=(fields, fields, fields, P(), blocks, blocks),
        out_specs=(fields, fields, fields),
        check_vma=False,
    )
```

```python
import functools

import jax
import jax.numpy as jnp
import numpy as np
from jax import lax
from jax.experimental import pallas as pl
from jax.experimental.pallas import tpu as pltpu
from jax.sharding import PartitionSpec as P

MESH = pl.DeviceIdType.MESH
F32 = jnp.float32
BF16 = jnp.bfloat16

lobatto_points = np.array(
    [
        -1.0,
        -0.8717401485096066,
        -0.5917001814331423,
        -0.2092992179024789,
        0.2092992179024789,
        0.5917001814331423,
        0.8717401485096066,
        1.0,
    ]
)
flux_half = 0.08
gamma_less = 0.4
acoustic_step = 0.01
upwind_speed = 1.5
face_lift = 28.0
REACH = 4
GREET = 4
ROWS = 64
WINDOW = 4


def derivative_matrix():
    points = lobatto_points
    gaps = points[:, None] - points[None, :] + np.eye(8)
    products = np.prod(gaps, axis=1)
    matrix = products[:, None] / (products[None, :] * gaps)
    np.fill_diagonal(matrix, 0.0)
    np.fill_diagonal(matrix, -matrix.sum(axis=1))
    return matrix


def derivative_operands():
    deriv = derivative_matrix()
    eye = np.eye(8)
    along_xy = np.concatenate([np.kron(deriv, eye), np.kron(eye, deriv)], axis=1)
    along_z = np.kron(np.eye(16), deriv.T)
    whole = np.concatenate([along_xy, along_z], axis=0).astype(np.float32)
    high = whole.astype(jnp.bfloat16)
    low = (whole - high.astype(np.float32)).astype(jnp.bfloat16)
    return np.stack([high, low])


def split(value):
    high = value.astype(BF16)
    return high, (value - high.astype(F32)).astype(BF16)


def dot_nn(left, right):
    return lax.dot_general(left, right, (((1,), (0,)), ((), ())), preferred_element_type=F32)


def dot_nt(left, right):
    return lax.dot_general(left, right, (((1,), (1,)), ((), ())), preferred_element_type=F32)


def lanes(shape):
    return lax.broadcasted_iota(jnp.int32, shape, len(shape) - 1)


def rows(shape):
    return lax.broadcasted_iota(jnp.int32, shape, len(shape) - 2)


class Halo:
    def __init__(self, x_ref, y_ref, z_ref, first):
        self.x_ref, self.y_ref, self.z_ref, self.first = x_ref, y_ref, z_ref, first

    def face(self, component, axis, side):
        at = self.first + component
        if axis == 0:
            return self.x_ref[side, at]
        if axis == 1:
            return self.y_ref[side, at]
        face = self.z_ref[side]
        return [jnp.broadcast_to(face[:, 8 * at + x : 8 * at + x + 1], (8, 128)) for x in range(8)]

    def shifted(self, field, component, axis, side):
        return shift(field, self.face(component, axis, side), axis, side)


def shift(field, face, axis, side):
    if axis == 0:
        if side == 0:
            return jnp.concatenate([face[None], field[:-1]], axis=0)
        return jnp.concatenate([field[1:], face[None]], axis=0)
    if axis == 1:
        rolled = pltpu.roll(field, 1 if side == 0 else 7, 1)
        edge = rows((8, 8, 128)) == (0 if side == 0 else 7)
        return jnp.where(edge, jnp.broadcast_to(face[:, None, :], (8, 8, 128)), rolled)
    rolled = pltpu.roll(field, 1 if side == 0 else 127, 2)
    edge = lanes((8, 8, 128)) == (0 if side == 0 else 127)
    return jnp.where(edge, jnp.stack(face), rolled)


def les_rate(state, halo):
    total = [-6.0 * part for part in state]
    for axis in range(3):
        for side in range(2):
            near = [halo.shifted(state[c], c, axis, side) for c in range(5)]
            momentum = near[1:4]
            energy = near[4] + 2.5
            inverse = 1.0 / (near[0] + 1.0)
            square = (
                momentum[0] * momentum[0] + momentum[1] * momentum[1] + momentum[2] * momentum[2]
            )
            pressure = gamma_less * (energy - 0.5 * (square * inverse))
            speed = momentum[axis] * inverse
            flux = [momentum[axis]]
            for component in range(3):
                term = momentum[component] * speed
                flux.append(term + pressure if component == axis else term)
            flux.append((energy + pressure) * speed)
            for c in range(5):
                total[c] = total[c] + (near[c] + flux[c] if side == 0 else near[c] - flux[c])
    return [flux_half * part for part in total]


def lamb_vector(state, halo):
    inverse = 1.0 / (state[0] + 1.0)
    velocity = [state[1 + c] * inverse for c in range(3)]
    packed = []
    for side in range(2):
        face = halo.z_ref[side]
        inverse_face = 1.0 / (face + 1.0)
        packed.append([face * pltpu.roll(inverse_face, 8 * (1 + c), 1) for c in range(3)])

    def near(component, axis, side):
        if axis == 2:
            face = packed[side][component]
            start = 8 * (1 + component)
            face = [jnp.broadcast_to(face[:, start + x : start + x + 1], (8, 128)) for x in range(8)]
        else:
            face = halo.face(1 + component, axis, side) / (halo.face(0, axis, side) + 1.0)
        return shift(velocity[component], face, axis, side)

    def slope(component, axis):
        return 0.5 * (near(component, axis, 1) - near(component, axis, 0))

    vort_x = slope(2, 1) - slope(1, 2)
    vort_y = slope(0, 2) - slope(2, 0)
    vort_z = slope(1, 0) - slope(0, 1)
    return [
        vort_y * velocity[2] - vort_z * velocity[1],
        vort_z * velocity[0] - vort_x * velocity[2],
        vort_x * velocity[1] - vort_y * velocity[0],
    ]


def flux_along(state, mean_speed, axis):
    flux = [mean_speed[axis] * state[0] + state[1 + axis]]
    for component in range(3):
        term = mean_speed[axis] * state[1 + component]
        flux.append(term + state[0] if component == axis else term)
    return flux


def acoustic_rate(state, mean_speed, halo, deriv_ref):
    flux_x = flux_along(state, mean_speed, 0)
    flux_y = flux_along(state, mean_speed, 1)
    flux_z = flux_along(state, mean_speed, 2)
    high = deriv_ref[0]
    low = deriv_ref[1]
    columns = jnp.concatenate(
        [
            jnp.concatenate([flux_x[c].reshape(64, 128), flux_y[c].reshape(64, 128)], axis=0)
            for c in range(4)
        ],
        axis=1,
    )
    column_high, column_low = split(columns)
    slopes_xy = (
        dot_nn(high[:64], column_high) + dot_nn(high[:64], column_low) + dot_nn(low[:64], column_high)
    )
    lines = jnp.concatenate([flux_z[c].reshape(64, 128) for c in range(4)], axis=0)
    line_high, line_low = split(lines)
    slopes_z = (
        dot_nn(line_high, high[64:]) + dot_nn(line_low, high[64:]) + dot_nn(line_high, low[64:])
    )
    total = [
        -(slopes_xy[:, 128 * c : 128 * c + 128] + slopes_z[64 * c : 64 * c + 64]).reshape(8, 8, 128)
        for c in range(4)
    ]
    half_lift = 0.5 * face_lift
    upwind_lift = half_lift * upwind_speed
    for side in range(2):
        plane = 0 if side == 0 else 7
        jump = [halo.face(c, 0, side) - state[c][plane] for c in range(4)]
        flux = flux_along(jump, [mean_speed[0][plane], None, None], 0)
        sign = half_lift if side == 0 else -half_lift
        for c in range(4):
            lifted = (sign * flux[c] + upwind_lift * jump[c])[None]
            zeros = jnp.zeros((7, 8, 128), F32)
            parts = [lifted, zeros] if side == 0 else [zeros, lifted]
            total[c] = total[c] + jnp.concatenate(parts, axis=0)
    for axis in (1, 2):
        position = rows((8, 8, 128)) if axis == 1 else lanes((8, 8, 128)) % 8
        is_left, is_right = position == 0, position == 7
        jump = []
        for c in range(4):
            if axis == 1:
                lower = jnp.broadcast_to(halo.face(c, 1, 0)[:, None, :], (8, 8, 128))
                upper = jnp.broadcast_to(halo.face(c, 1, 1)[:, None, :], (8, 8, 128))
            else:
                lower = halo.shifted(state[c], c, 2, 0)
                upper = halo.shifted(state[c], c, 2, 1)
            other = jnp.where(is_left, lower, jnp.where(is_right, upper, state[c]))
            jump.append(other - state[c])
        flux = flux_along(jump, mean_speed, axis)
        sign = jnp.where(is_left, half_lift, -half_lift)
        for c in range(4):
            total[c] = total[c] + (sign * flux[c] + upwind_lift * jump[c])
    return total


def pack_faces_z(planes, side):
    return pack_lane(planes, 127 * side, 0)


def pack_lane(planes, at, first):
    face = jnp.zeros((8, 128), F32)
    lane = lanes((8, 128))
    for n, plane in enumerate(planes, first):
        face = jnp.where(lane == n, jnp.broadcast_to(plane[:, at : at + 1], (8, 128)), face)
    return face


def quarter_transpose(groups, target):
    lane = lanes(groups[0].shape) // 32
    result = None
    for g, group in enumerate(groups):
        moved = group if g == target else pltpu.roll(group, (32 * (g - target)) % 128, 1)
        result = moved if result is None else jnp.where(lane == g, moved, result)
    return result


def projection_operands(proj_ref):
    lane = lanes((8, 128))
    row = rows((8, 128))
    tile = jnp.zeros((8, 128), F32)
    for k in range(8):
        for e in range(8):
            tile = jnp.where((row == k) & (lane % 8 == e), proj_ref[k, e], tile)
    pieces = []
    for i in range(8):
        weight = jnp.zeros((8, 128), F32)
        for a in range(8):
            weight = jnp.where(lane % 64 // 8 == a, proj_ref[i, a], weight)
        pieces.append(weight * tile)
    return tile, jnp.concatenate(pieces, axis=0)


def place_operands(tile, own_ref, slot_ref, start):
    lane = lanes((8, 128))
    row = rows((8, 128))
    block = lane // 8
    owner = jnp.zeros((8, 128), jnp.int32)
    slot = jnp.zeros((8, 128), jnp.int32)
    for b in range(16):
        owner = jnp.where(block == b, own_ref[0, 0, b], owner)
        slot = jnp.where(block == b, slot_ref[0, 0, b], slot)
    rank = jnp.zeros((8, 128), jnp.int32)
    for b in range(16):
        rank = rank + jnp.where((owner == own_ref[0, 0, b]) & (block > b), 1, 0)
    place = (owner - start) * WINDOW + rank
    columns = jnp.concatenate([jnp.where(place == n, tile, 0.0) for n in range(16)], axis=0)
    same = (lane % 8) == row
    picks = jnp.concatenate(
        [jnp.where((place == n) & same, 1.0, 0.0) for n in range(16)], axis=0
    )
    labels = dot_nt(slot.astype(F32).astype(BF16), picks.astype(BF16))
    return columns, labels


def kernel(
    sizes,
    les,
    ac,
    mf,
    proj_hbm,
    own_hbm,
    slot_hbm,
    deriv,
    les_next,
    src_v,
    ac_next,
    proj,
    own,
    slot,
    les_v,
    ac_v,
    mf_v,
    deriv_v,
    send_y,
    send_z,
    halo_x,
    halo_y,
    halo_z,
    pieces,
    arrived,
    sec_v,
    sec_send_y,
    sec_send_z,
    sec_halo_x,
    sec_halo_y,
    sec_halo_z,
    mid_v,
    mid_send_y,
    mid_send_z,
    mid_halo_x,
    mid_halo_y,
    mid_halo_z,
    placed_v,
    side_tiles,
    side_arrived,
    end_rows,
    end_arrived,
    rate_v,
    slope_v,
    load_sem,
    send_sem,
    recv_sem,
    piece_send,
    piece_recv,
    side_send,
    side_recv,
):
    names = ("gx", "gy", "gz")
    at = [lax.axis_index(name) for name in names]
    me = at[0]
    count_x = sizes[0]

    def exists(axis, distance):
        other = at[axis] + distance
        return (other >= 0) & (other < sizes[axis])

    barrier = pltpu.get_barrier_semaphore()
    expected = jnp.int32(0)
    for axis, reach in ((0, GREET), (1, 1), (2, 1)):
        for distance in sorted(range(-reach, reach + 1), key=abs):
            if distance == 0:
                continue
            near = exists(axis, distance)

            @pl.when(near)
            def _():
                pl.semaphore_signal(
                    barrier,
                    inc=1,
                    device_id={names[axis]: at[axis] + distance},
                    device_id_type=MESH,
                )

            expected = expected + jnp.where(near, 1, 0)

    loads = [
        pltpu.make_async_copy(source, target, load_sem.at[n])
        for n, (source, target) in enumerate(
            (
                (les, les_v),
                (ac, ac_v),
                (proj_hbm, proj),
                (own_hbm, own),
                (slot_hbm, slot),
                (mf, mf_v),
                (deriv, deriv_v),
            )
        )
    ]
    for load in loads:
        load.start()

    def start_of(index):
        return (index * (count_x - (WINDOW - 1))) // count_x

    start = start_of(me)

    def comes(distance):
        other = me + distance
        begin = start_of(other)
        return exists(0, distance) & (begin <= me) & (me < begin + WINDOW)

    def grazes(distance):
        begin = start_of(me + distance)
        return exists(0, distance) & ((me + 1 == begin) | (me == begin + WINDOW))

    for side, distance in ((0, -1), (1, 1)):
        for axis, refs in (
            (0, (halo_x, sec_halo_x, mid_halo_x)),
            (1, (halo_y, sec_halo_y, mid_halo_y)),
            (2, (halo_z, sec_halo_z, mid_halo_z)),
        ):

            @pl.when(jnp.logical_not(exists(axis, distance)))
            def _():
                for ref in refs:
                    ref[side] = jnp.zeros(ref.shape[1:], F32)

    for distance in range(-REACH, REACH + 1):
        if distance != 0:

            grazed, other = (56, 48) if distance > 0 else (48, 56)

            @pl.when(jnp.logical_not(comes(distance)))
            def _():
                arrived[distance + REACH, 0:48] = jnp.zeros((48, 128), F32)
                arrived[distance + REACH, other : other + 8] = jnp.zeros((8, 128), F32)

            @pl.when(jnp.logical_not(comes(distance) | grazes(distance)))
            def _():
                arrived[distance + REACH, grazed : grazed + 8] = jnp.zeros((8, 128), F32)

    def side_of(n):
        return 1 + n // 2, 2 * (n % 2) - 1

    def side_comes(n, distance):
        return exists(*side_of(n)) & comes(distance)

    for n in range(4):
        for distance in range(-3, 4):

            @pl.when(jnp.logical_not(side_comes(n, distance)))
            def _():
                if n < 2:
                    side_arrived[n, distance + 3] = jnp.zeros((8, 128), F32)
                else:
                    end_arrived[n - 2, distance + 3] = jnp.zeros((1, 256), F32)

    def message(source, target, axis, side, slot_index):
        distance = -1 if side == 0 else 1
        return pltpu.make_async_remote_copy(
            src_ref=source,
            dst_ref=target,
            send_sem=send_sem.at[slot_index],
            recv_sem=recv_sem.at[slot_index],
            device_id={names[axis]: at[axis] + distance},
            device_id_type=MESH,
        )

    def begin(entries):
        for source, target, axis, side, slot_index in entries:

            @pl.when(exists(axis, -1 if side == 0 else 1))
            def _():
                message(source, target, axis, side, slot_index).start()

    def arrive(entries):
        for source, target, axis, side, slot_index in entries:
            @pl.when(exists(axis, 1 if side == 0 else -1))
            def _():
                message(source, target, axis, side, slot_index).wait_recv()

    def drain(entries):
        for source, target, axis, side, slot_index in entries:

            @pl.when(exists(axis, -1 if side == 0 else 1))
            def _():
                message(source, target, axis, side, slot_index).wait_send()

    flow_x = [
        (les_v.at[:, 0 if side == 0 else 7], halo_x.at[1 - side, 0:5], 0, side, side)
        for side in range(2)
    ]
    flow_y = [
        (send_y.at[side, 0:5], halo_y.at[1 - side, 0:5], 1, side, 4 + side) for side in range(2)
    ]
    both_z = [(send_z.at[side], halo_z.at[1 - side], 2, side, 6 + side) for side in range(2)]
    sound = [
        (ac_v.at[:, 0 if side == 0 else 7], halo_x.at[1 - side, 5:9], 0, side, 2 + side)
        for side in range(2)
    ] + [
        (send_y.at[side, 5:9], halo_y.at[1 - side, 5:9], 1, side, 20 + side) for side in range(2)
    ]
    section = (
        [
            (sec_v.at[:, 0 if side == 0 else 7], sec_halo_x.at[1 - side], 0, side, 8 + side)
            for side in range(2)
        ]
        + [
            (sec_send_y.at[side], sec_halo_y.at[1 - side], 1, side, 10 + side)
            for side in range(2)
        ]
        + [
            (sec_send_z.at[side], sec_halo_z.at[1 - side], 2, side, 12 + side)
            for side in range(2)
        ]
    )
    middle = (
        [
            (mid_v.at[:, 0 if side == 0 else 7], mid_halo_x.at[1 - side], 0, side, 14 + side)
            for side in range(2)
        ]
        + [
            (mid_send_y.at[side], mid_halo_y.at[1 - side], 1, side, 16 + side)
            for side in range(2)
        ]
        + [
            (mid_send_z.at[side], mid_halo_z.at[1 - side], 2, side, 18 + side)
            for side in range(2)
        ]
    )

    for load in loads[:2]:
        load.wait()
    for side in range(2):
        row = 0 if side == 0 else 7
        send_y[side, 0:5] = les_v[:, :, row, :]
        send_y[side, 5:9] = ac_v[:, :, row, :]
        send_z[side] = pack_faces_z(
            [les_v[c, x] for c in range(5) for x in range(8)]
            + [ac_v[c, x] for c in range(4) for x in range(8)],
            side,
        )

    pl.semaphore_wait(barrier, expected)
    begin(flow_x)
    begin(flow_y)
    begin(both_z)
    begin(sound)
    for load in loads[2:]:
        load.wait()

    tile, plane_weights = projection_operands(proj)
    weight_high, weight_low = split(plane_weights)
    plane_operand = jnp.concatenate([weight_high, weight_low], axis=1)
    columns, labels = place_operands(tile, own, slot, start)
    column_high, column_low = split(columns)
    column_operand = jnp.concatenate(
        [
            jnp.concatenate([column_high, column_high], axis=1),
            jnp.concatenate([column_low, column_low], axis=1),
        ],
        axis=0,
    )
    state = [les_v[c] for c in range(5)]
    halo = Halo(halo_x, halo_y, halo_z, 0)
    arrive(flow_y)
    arrive(both_z)
    arrive(flow_x)
    lamb = lamb_vector(state, halo)
    cells = jnp.concatenate([part.reshape(64, 128) for part in lamb], axis=1)
    cell_high, cell_low = split(cells)
    stacked = jnp.concatenate([cell_high, cell_low, cell_high, cell_low], axis=0)
    planes = dot_nn(plane_operand, stacked)
    planes = jnp.concatenate([planes[:, 128 * c : 128 * c + 128] for c in range(3)], axis=0)
    plane_high, plane_low = split(planes)
    both = dot_nt(jnp.concatenate([plane_high, plane_low], axis=1), column_operand)
    placed = both[:, :128] + both[:, 128:]
    groups = [placed[48 * g : 48 * g + 48] for g in range(4)]
    lows = [placed[64 * c : 64 * c + 8] for c in range(3)] + [labels]
    highs = [placed[64 * c + 56 : 64 * c + 64] for c in range(3)] + [labels]
    for w in range(WINDOW):
        pieces[w + 1, 0:48] = quarter_transpose(groups, w)
    lane = lanes((8, 128))
    row = rows((8, 128))
    for w in range(-1, WINDOW + 1):
        zero = jnp.zeros((8, 128), F32)
        above = quarter_transpose(highs, w - 1) if w >= 1 else zero
        below = quarter_transpose(lows, w + 1) if w + 1 < WINDOW else zero
        if 0 <= w < WINDOW:
            moved = labels if w == 3 else pltpu.roll(labels, 32 * (3 - w), 1)
            above = jnp.where((lane >= 96) & (row >= 4), moved, above)
        pieces[w + 1, 48:56] = above
        pieces[w + 1, 56:64] = below

    def piece_copy(w):
        target = start + w
        slot_index = me - target + REACH
        return pltpu.make_async_remote_copy(
            src_ref=pieces.at[w + 1],
            dst_ref=arrived.at[slot_index],
            send_sem=piece_send.at[w + 1],
            recv_sem=piece_recv.at[slot_index],
            device_id={"gx": target},
            device_id_type=MESH,
        )

    def edge_copy(w):
        target = start + w
        slot_index = me - target + REACH
        part = slice(56, 64) if w < 0 else slice(48, 56)
        return pltpu.make_async_remote_copy(
            src_ref=pieces.at[w + 1, part],
            dst_ref=arrived.at[slot_index, part],
            send_sem=piece_send.at[w + 1],
            recv_sem=piece_recv.at[slot_index],
            device_id={"gx": target},
            device_id_type=MESH,
        )

    @pl.when(start >= 1)
    def _():
        edge_copy(-1).start()

    @pl.when(start + WINDOW < count_x)
    def _():
        edge_copy(WINDOW).start()

    for w in range(WINDOW):

        @pl.when(start + w != me)
        def _():
            piece_copy(w).start()

    arrived[REACH] = pieces[me - start + 1]

    def side_copy(n, w):
        axis, distance = side_of(n)
        target = start + w
        slot_index = me - target + 3
        landing = n + 1 - 2 * (n % 2)
        if n < 2:
            source, goal = side_tiles.at[n, w], side_arrived.at[landing, slot_index]
        else:
            source, goal = end_rows.at[4 * (n - 2) + w], end_arrived.at[landing - 2, slot_index]
        return pltpu.make_async_remote_copy(
            src_ref=source,
            dst_ref=goal,
            send_sem=side_send.at[4 * n + w],
            recv_sem=side_recv.at[7 * landing + slot_index],
            device_id={"gx": target, names[axis]: at[axis] + distance},
            device_id_type=MESH,
        )

    def side_begin(n):
        @pl.when(exists(*side_of(n)))
        def _():
            for w in range(WINDOW):
                side_copy(n, w).start()

    placed_v[...] = placed.reshape(3, 8, 8, 128)
    for n in range(2):
        parts = [placed_v[c, :, 7 * n, :] for c in range(3)] + [labels]
        for w in range(WINDOW):
            side_tiles[n, w] = quarter_transpose(parts, w)
        side_begin(n)
    upper = row >= 4
    wanted = (
        (lane // 32 == row % 4)
        & (lane % 8 == jnp.where(upper, 7, 0))
        & (labels == jnp.where(upper, 15.0, 0.0))
    )
    ends = jnp.where(wanted, 1.0, 0.0).astype(BF16)
    placed_high, placed_low = split(
        jnp.concatenate([placed, jnp.zeros((64, 128), F32)], axis=0)
    )
    sums = dot_nt(ends, placed_high) + dot_nt(ends, placed_low)
    for n in range(8):
        end_rows[n] = sums[n : n + 1]
    side_begin(2)
    side_begin(3)

    rate = les_rate(state, halo)
    for c in range(5):
        rate_v[c] = rate[c]
        sec_v[c] = state[c] + rate[c]
    for side in range(2):
        sec_send_y[side] = sec_v[:, :, 0 if side == 0 else 7, :]
        sec_send_z[side] = pack_faces_z(
            [sec_v[c, x] for c in range(5) for x in range(8)], side
        )
    begin(section)

    mean_speed = [mf_v[c] for c in range(3)]
    arrive(sound)
    slopes = acoustic_rate(
        [ac_v[c] for c in range(4)], mean_speed, Halo(halo_x, halo_y, halo_z, 5), deriv_v
    )
    for c in range(4):
        slope_v[c] = slopes[c]
        mid_v[c] = ac_v[c] + acoustic_step * slopes[c]
    for side in range(2):
        mid_send_y[side] = mid_v[:, :, 0 if side == 0 else 7, :]
        mid_send_z[side] = pack_faces_z([mid_v[c, x] for c in range(4) for x in range(8)], side)
    begin(middle)
    drain(flow_x)
    drain(flow_y)
    drain(both_z)
    drain(sound)

    for distance in range(-REACH, REACH + 1):
        if distance != 0:

            @pl.when(comes(distance))
            def _():
                pltpu.make_async_remote_copy(
                    src_ref=pieces.at[0],
                    dst_ref=arrived.at[distance + REACH],
                    send_sem=piece_send.at[0],
                    recv_sem=piece_recv.at[distance + REACH],
                    device_id={"gx": me + distance},
                    device_id_type=MESH,
                ).wait_recv()

            @pl.when(grazes(distance))
            def _():
                part = slice(56, 64) if distance > 0 else slice(48, 56)
                pltpu.make_async_remote_copy(
                    src_ref=pieces.at[0, part],
                    dst_ref=arrived.at[distance + REACH, part],
                    send_sem=piece_send.at[0],
                    recv_sem=piece_recv.at[distance + REACH],
                    device_id={"gx": me + distance},
                    device_id_type=MESH,
                ).wait_recv()

    same = (lanes((8, 128)) % 8) == rows((8, 128))

    def picks_of(tags):
        return jnp.concatenate(
            [
                jnp.concatenate(
                    [jnp.where((tag == float(n)) & same, 1.0, 0.0) for n in range(16)], axis=0
                )
                for tag in tags
            ],
            axis=1,
        ).astype(BF16)

    def gather(halves, tags):
        picks = picks_of(tags)
        high, low = split(jnp.concatenate(halves, axis=1))
        return dot_nt(high, picks) + dot_nt(low, picks)

    def members_of(half, first, part):
        members = [first + REACH + 4 * half + n for n in range(4)]
        zero = jnp.zeros((part.stop - part.start, 128), F32)
        return [arrived[n, part] if 4 * half + k < 7 else zero for k, n in enumerate(members)]

    halves, tags = [], []
    for half in range(2):
        parts = members_of(half, -3, slice(0, 48))
        halves.append(
            jnp.concatenate([quarter_transpose(parts, g) for g in range(4)], axis=0)
        )
        tag = quarter_transpose(members_of(half, -3, slice(48, 56)), 3)
        tags.append(jnp.broadcast_to(tag[4:5], (8, 128)))
    src_v[...] = gather(halves, tags).reshape(3, 8, 8, 128)
    for n in range(4):
        for distance in range(-3, 4):

            @pl.when(side_comes(n, distance))
            def _():
                axis, step = side_of(n)
                if n < 2:
                    source, goal = side_tiles.at[0, 0], side_arrived.at[n, distance + 3]
                else:
                    source, goal = end_rows.at[0], end_arrived.at[n - 2, distance + 3]
                pltpu.make_async_remote_copy(
                    src_ref=source,
                    dst_ref=goal,
                    send_sem=side_send.at[0],
                    recv_sem=side_recv.at[7 * n + distance + 3],
                    device_id={"gx": me + distance, names[axis]: at[axis] + step},
                    device_id_type=MESH,
                ).wait_recv()


    def gather_tiles(tiles):
        halves, tags = [], []
        for parts in (tiles[:4], tiles[4:] + [jnp.zeros((8, 128), F32)]):
            halves.append(
                jnp.concatenate([quarter_transpose(parts, c) for c in range(3)], axis=0)
            )
            tag = quarter_transpose(parts, 3)
            tags.append(jnp.broadcast_to(tag[0:1], (8, 128)))
        return gather(halves, tags)

    source_x = [
        gather_tiles([arrived[first + n, part] for n in range(7)])
        for first, part in ((0, slice(48, 56)), (2, slice(56, 64)))
    ]
    line = lax.broadcasted_iota(jnp.int32, (256, 128), 0)
    folds = jnp.where(lanes((256, 128)) == 8 + line // 8, 1.0, 0.0).astype(BF16)
    source_z = []
    for side in range(2):
        line_sum = end_arrived[side, 0]
        for n in range(1, 7):
            line_sum = line_sum + end_arrived[side, n]
        spread = jnp.broadcast_to(line_sum, (8, 256))
        spread = jnp.where(lanes((8, 256)) % 8 == rows((8, 256)), spread, 0.0)
        spread_high, spread_low = split(spread)
        source_z.append(dot_nn(spread_high, folds) + dot_nn(spread_low, folds))
    source_y = [gather_tiles([side_arrived[side, n] for n in range(7)]) for side in range(2)]

    arrive(section)
    rate = les_rate([sec_v[c] for c in range(5)], Halo(sec_halo_x, sec_halo_y, sec_halo_z, 0))
    for c in range(5):
        les_next[c] = les_v[c] + 0.5 * (rate_v[c] + rate[c])

    arrive(middle)
    for side in range(2):
        mid_halo_z[side] = mid_halo_z[side] + acoustic_step * source_z[side]
        for c in range(3):
            for ref, face in ((mid_halo_x, source_x[side]), (mid_halo_y, source_y[side])):
                ref[side, 1 + c] = ref[side, 1 + c] + acoustic_step * face[8 * c : 8 * c + 8]
    slopes = acoustic_rate(
        [mid_v[0]] + [mid_v[1 + c] + acoustic_step * src_v[c] for c in range(3)],
        mean_speed,
        Halo(mid_halo_x, mid_halo_y, mid_halo_z, 0),
        deriv_v,
    )
    for c in range(4):
        total = slope_v[c] + slopes[c]
        if c > 0:
            total = total + 2.0 * src_v[c - 1]
        ac_next[c] = ac_v[c] + 0.5 * acoustic_step * total

    drain(section)
    drain(middle)

    for n in range(4):

        @pl.when(exists(*side_of(n)))
        def _():
            for w in range(WINDOW):
                side_copy(n, w).wait_send()

    @pl.when(start >= 1)
    def _():
        edge_copy(-1).wait_send()

    @pl.when(start + WINDOW < count_x)
    def _():
        edge_copy(WINDOW).wait_send()

    for w in range(WINDOW):

        @pl.when(start + w != me)
        def _():
            piece_copy(w).wait_send()


def write_out(les_v, src_v, ac_v, les_out, src_out, ac_out, sems):
    copies = [
        pltpu.make_async_copy(source, target, sems.at[n])
        for n, (source, target) in enumerate(((les_v, les_out), (src_v, src_out), (ac_v, ac_out)))
    ]
    for copy in copies:
        copy.start()
    for copy in copies:
        copy.wait()


def local(les_state, acoustic_state, mean_flow, projection, target_owner, target_slot):
    sizes = tuple(lax.axis_size(name) for name in ("gx", "gy", "gz"))
    deriv = jnp.asarray(derivative_operands())
    anywhere = pl.BlockSpec(memory_space=pl.ANY)
    scalars = pl.BlockSpec(memory_space=pltpu.SMEM)

    def vmem(*shape):
        return pltpu.VMEM(shape, F32)

    def halos(n):
        return [vmem(2, n, 8, 128), vmem(2, n, 8, 128), vmem(2, 8, 128)]

    field = (8, 8, 128)
    shapes = [(5,) + field, (3,) + field, (4,) + field]
    on_chip = pl.BlockSpec(memory_space=pltpu.VMEM)
    results = pl.pallas_call(
        functools.partial(kernel, sizes),
        name="coupled_step",
        out_shape=tuple(pltpu.VMEM(shape, F32) for shape in shapes),
        in_specs=[anywhere] * 7,
        out_specs=(on_chip,) * 3,
        scratch_shapes=[
            pltpu.SMEM((8, 8), F32),
            pltpu.SMEM((1, 1, 16), jnp.int32),
            pltpu.SMEM((1, 1, 16), jnp.int32),
            vmem(5, *field),
            vmem(4, *field),
            vmem(3, *field),
            pltpu.VMEM((2, 192, 128), BF16),
            vmem(2, 9, 8, 128),
            vmem(2, 8, 128),
            *halos(9),
            vmem(6, ROWS, 128),
            vmem(9, ROWS, 128),
            vmem(5, *field),
            vmem(2, 5, 8, 128),
            vmem(2, 8, 128),
            *halos(5),
            vmem(4, *field),
            vmem(2, 4, 8, 128),
            vmem(2, 8, 128),
            *halos(4),
            vmem(3, *field),
            vmem(2, 4, 8, 128),
            vmem(2, 7, 8, 128),
            vmem(8, 1, 256),
            vmem(2, 7, 1, 256),
            vmem(5, *field),
            vmem(4, *field),
            pltpu.SemaphoreType.DMA((7,)),
            pltpu.SemaphoreType.DMA((22,)),
            pltpu.SemaphoreType.DMA((22,)),
            pltpu.SemaphoreType.DMA((6,)),
            pltpu.SemaphoreType.DMA((9,)),
            pltpu.SemaphoreType.DMA((16,)),
            pltpu.SemaphoreType.DMA((28,)),
        ],
        compiler_params=pltpu.CompilerParams(collective_id=0, has_side_effects=True),
    )(les_state, acoustic_state, mean_flow, projection, target_owner, target_slot, deriv)
    return pl.pallas_call(
        write_out,
        name="write_out",
        out_shape=tuple(jax.ShapeDtypeStruct(shape, F32) for shape in shapes),
        in_specs=[on_chip] * 3,
        out_specs=(anywhere,) * 3,
        scratch_shapes=[pltpu.SemaphoreType.DMA((3,))],
    )(*[pltpu.with_memory_space_constraint(result, pltpu.VMEM) for result in results])


def solution(mesh):
    fields = P(None, "gx", "gy", "gz")
    blocks = P("gx", "gy", "gz")
    return jax.shard_map(
        local,
        mesh=mesh,
        in_specs=(fields, fields, fields, P(), blocks, blocks),
        out_specs=(fields, fields, fields),
        check_vma=False,
    )
```
